32 devices in a mesh: group: 2 (over y), shard: 4 (over x, core), ctx: 4 (over z).
Axes of the slice: x: 2, y: 2, z: 4, core: 2. Of those that a mesh axis runs over, the one named last changes fastest.
Arguments:
- inputs: bfloat16 [8, 1024, 768], P(('group', 'shard'), 'ctx'), may hold values from -6 to 6
- doc_lengths: int32 [8, 5], P(('group', 'shard')), may hold values from 1 to 512, 1024 in all within a row
- query_weight: bfloat16 [768, 768], P('shard'), may hold values from -0.21875 to 0.21875
- key_weight: bfloat16 [768, 768], P('shard'), may hold values from -0.21875 to 0.21875
- value_weight: bfloat16 [768, 768], P('shard'), may hold values from -0.21875 to 0.21875
- out_weight: bfloat16 [768, 768], P('shard'), may hold values from -0.875 to 0.875
- query_bias: bfloat16 [768], P('shard'), may hold values from -3 to 3
- key_bias: bfloat16 [768], P('shard'), may hold values from -3 to 3
- value_bias: bfloat16 [768], P('shard'), may hold values from -3 to 3
- out_bias: bfloat16 [768], P('shard'), may hold values from -3 to 3
- first_gain: bfloat16 [768], P('shard'), may hold values from 0.5 to 1.5
- first_shift: bfloat16 [768], P('shard'), may hold values from -2 to 2
- up_weight: bfloat16 [768, 3072], P('shard'), may hold values from -0.21875 to 0.21875
- up_bias: bfloat16 [3072], P('shard'), may hold values from -3 to 3
- down_weight: bfloat16 [3072, 768], P('shard'), may hold values from -0.21875 to 0.21875
- down_bias: bfloat16 [768], P('shard'), may hold values from -3 to 3
- second_gain: bfloat16 [768], P('shard'), may hold values from 0.5 to 1.5
- second_shift: bfloat16 [768], P('shard'), may hold values from -2 to 2
- cotangent: bfloat16 [8, 1024, 768], P(('group', 'shard'), 'ctx'), may hold values from -6 to 6
Outputs:
- output: bfloat16 [8, 1024, 768], P(('group', 'shard'), 'ctx')
- input_gradient: float32 [8, 1024, 768], P(('group', 'shard'), 'ctx')
- query_weight_gradient: float32 [768, 768], P('shard')
- key_weight_gradient: float32 [768, 768], P('shard')
- value_weight_gradient: float32 [768, 768], P('shard')
- out_weight_gradient: float32 [768, 768], P('shard')
- query_bias_gradient: float32 [768], P('shard')
- key_bias_gradient: float32 [768], P('shard')
- value_bias_gradient: float32 [768], P('shard')
- out_bias_gradient: float32 [768], P('shard')
- first_gain_gradient: float32 [768], P('shard')
- first_shift_gradient: float32 [768], P('shard')
- up_weight_gradient: float32 [768, 3072], P('shard')
- up_bias_gradient: float32 [3072], P('shard')
- down_weight_gradient: float32 [3072, 768], P('shard')
- down_bias_gradient: float32 [768], P('shard')
- second_gain_gradient: float32 [768], P('shard')
- second_shift_gradient: float32 [768], P('shard')
The draws below stay inside these ranges and needn't reach their ends.
Inputs may be any that keep to these rules, and one draw needn't show every extreme that they name: `doc_lengths`: each stream's document lengths sum to 1024, and the longest of each stream is exactly 512.
All inputs are finite; a program needn't handle non-finite values.
Results may differ from the reference program's by a relative error of at most 0.017.
Values may be sent and summed in bfloat16 or wider, within the bound.
No kernel may reach another device: no remote copies, remote signals or barrier semaphores. Data moves between devices by JAX's collectives and lax.ppermute only.
A program may use at most 128 MiB of HBM per device.

```python
import math
from functools import partial
import jax
import jax.numpy as jnp
import numpy as np
from jax import lax

D = 768
HEAD = 64
FF = 3072
SEQ = 1024
STREAMS = 8
MAXDOC = 512
NDOC = 5


def level_of(rng, extent, cuts, least, largest):
    level = 1.0
    for position, shards_of in cuts:
        steps = jax.random.uniform(jax.random.fold_in(jax.random.fold_in(rng, 6), position), (shards_of,), jnp.float32, least / len(cuts), largest / len(cuts))
        level = level * jnp.repeat(jnp.exp(steps), extent[position] // shards_of).reshape((-1,) + (1,) * (len(extent) - 1 - position))
    return level


def length_profile(amount, total, bound, skew):
    portions = [(1 << 20) // math.isqrt(standing ** skew) + 1 for standing in range(2, amount + 1)]
    surplus, given = total - bound - (amount - 1), [1] * (amount - 1)
    while surplus > 0:
        free = [i for i in range(amount - 1) if given[i] < bound]
        mass, remaining = sum([portions[i] for i in free]), surplus
        for i in free:
            more = min(bound - given[i], max(1, remaining * portions[i] // mass), surplus)
            given[i] = given[i] + more
            surplus = surplus - more
    return np.array([bound] + given)


def uneven_parts(rng, number_of, total, bound, slope):
    if number_of == 2:
        one = jax.random.randint(rng, (), max(1, total - bound), min(bound, total - 1) + 1)
        return jnp.stack([one, total - one])
    tallies = jnp.asarray(length_profile(number_of, total, bound, slope), jnp.int32)
    twos = (number_of - 1) // 2
    source_of, sink = tallies[1:1 + 2 * twos:2], tallies[2:2 + 2 * twos:2]
    margin = jnp.minimum(source_of - 1, bound - sink)
    shifted = jax.random.randint(jax.random.fold_in(rng, 1), (twos,), 0, 1 << 20) % (margin + 1)
    tallies = tallies.at[1:1 + 2 * twos:2].set(source_of - shifted).at[2:2 + 2 * twos:2].set(sink + shifted)
    return tallies[jax.random.permutation(jax.random.fold_in(rng, 2), number_of)]


def gaussian(own_key, dims, scale, limit, cuts=(), kind=jnp.bfloat16):
    entries = jax.random.normal(own_key, dims, jnp.float32) * scale
    if len(cuts) > 0:
        entries = level_of(own_key, dims, cuts, -0.22, 0.18) * entries
    return jnp.clip(entries, min=-limit, max=limit).astype(kind)


def setup_inputs(seed: int = 0) -> dict:
    seeds = jax.random.split(jax.random.key(seed), 20)
    inputs = gaussian(seeds[0], (STREAMS, SEQ, D), 1.0, 6.0, ((0, 8), (1, 4)))
    doc_lengths = jax.vmap(lambda own: uneven_parts(own, NDOC, SEQ, MAXDOC, 2))(jax.random.split(seeds[1], STREAMS)).reshape((STREAMS, NDOC)).astype(jnp.int32)
    query_weight = gaussian(seeds[2], (D, D), D ** -0.5, 0.21875, ((0, 4),))
    key_weight = gaussian(seeds[3], (D, D), D ** -0.5, 0.21875, ((0, 4),))
    value_weight = gaussian(seeds[4], (D, D), D ** -0.5, 0.21875, ((0, 4),))
    out_weight = gaussian(seeds[5], (D, D), (D // 16) ** -0.5, 0.875, ((0, 4),))
    query_bias = gaussian(seeds[6], (D,), 0.5, 3.0, ((0, 4),))
    key_bias = gaussian(seeds[7], (D,), 0.5, 3.0, ((0, 4),))
    value_bias = gaussian(seeds[8], (D,), 0.5, 3.0, ((0, 4),))
    out_bias = gaussian(seeds[9], (D,), 0.5, 3.0, ((0, 4),))
    first_gain = jnp.clip(1.0 + 0.1 * jax.random.normal(seeds[10], (D,), jnp.float32), 0.5, 1.5).astype(jnp.bfloat16)
    first_shift = gaussian(seeds[11], (D,), 0.3, 2.0, ((0, 4),))
    up_weight = gaussian(seeds[12], (D, FF), D ** -0.5, 0.21875, ((0, 4),))
    up_bias = gaussian(seeds[13], (FF,), 0.5, 3.0, ((0, 4),))
    down_weight = gaussian(seeds[14], (FF, D), (FF // 4) ** -0.5, 0.21875, ((0, 4),))
    down_bias = gaussian(seeds[15], (D,), 0.5, 3.0, ((0, 4),))
    second_gain = jnp.clip(1.0 + 0.1 * jax.random.normal(seeds[16], (D,), jnp.float32), 0.5, 1.5).astype(jnp.bfloat16)
    second_shift = gaussian(seeds[17], (D,), 0.3, 2.0, ((0, 4),))
    cotangent = gaussian(seeds[18], (STREAMS, SEQ, D), 1.0, 6.0, ((0, 8), (1, 4)))
    return dict(inputs=inputs, doc_lengths=doc_lengths, query_weight=query_weight, key_weight=key_weight, value_weight=value_weight, out_weight=out_weight, query_bias=query_bias, key_bias=key_bias, value_bias=value_bias, out_bias=out_bias, first_gain=first_gain, first_shift=first_shift, up_weight=up_weight, up_bias=up_bias, down_weight=down_weight, down_bias=down_bias, second_gain=second_gain, second_shift=second_shift, cotangent=cotangent)


EPSILON = 1e-05

@jax.custom_vjp
def low(v):
    return lax.optimization_barrier(v.astype(jnp.bfloat16)).astype(jnp.float32)

@jax.custom_vjp
def low_back(v):
    return v

def low_keep(v):
    return (low(v), None)

def low_pass(kept, grad):
    return (grad,)

def back_keep(v):
    return (v, None)

def back_low(kept, grad):
    return (low(grad),)
low.defvjp(low_keep, low_pass)
low_back.defvjp(back_keep, back_low)

def matmul(left, right):
    return jnp.dot(left, right, precision=lax.Precision.HIGHEST)

def layer_norm(value, gain, shift):
    mean_value = lax.optimization_barrier(jnp.mean(value, axis=-1, keepdims=True))
    centred = value - mean_value
    variance = lax.optimization_barrier(jnp.mean(centred * centred, axis=-1, keepdims=True))
    return centred * lax.rsqrt(variance + EPSILON) * gain + shift

def rope_angles(places):
    half_width = HEAD // 2
    freqs = 10000.0 ** (-jnp.arange(half_width, dtype=jnp.float32) * (2.0 / HEAD))
    angles = places[:, None] * freqs[None, :]
    return (jnp.cos(angles), jnp.sin(angles))

def rotate(value, cosine, sine):
    count = value.shape[0]
    split = value.reshape(count, -1, HEAD // 2, 2)
    first = split[:, :, :, 0]
    second = split[:, :, :, 1]
    cosine_b = cosine[:, None, :]
    sine_b = sine[:, None, :]
    turned = jnp.stack([first * cosine_b - second * sine_b, second * cosine_b + first * sine_b], axis=3)
    return turned.reshape(count, -1)

def document_tables(lengths):
    starts = jnp.cumsum(lengths) - lengths
    places = jnp.arange(SEQ, dtype=jnp.int32)
    before = starts[None, :] <= places[:, None]
    counted = lax.optimization_barrier(jnp.sum(before.astype(jnp.int32), axis=1))
    first_place = lax.optimization_barrier(jnp.max(jnp.where(before, starts[None, :], 0), axis=1))
    same_doc = counted[:, None] == counted[None, :]
    cosine, sine = rope_angles((places - first_place).astype(jnp.float32))
    return (same_doc, cosine, sine)

def head_attention(same_doc, packed):
    query, key, value = packed
    scores = low_back(matmul(query, key.T) * HEAD ** (-0.5))
    scores = jnp.where(same_doc, scores, -jnp.inf)
    peak = lax.optimization_barrier(jnp.max(scores, axis=1, keepdims=True))
    expo = jnp.exp(scores - peak)
    probs = low(expo / lax.optimization_barrier(jnp.sum(expo, axis=1, keepdims=True)))
    return matmul(probs, value)

def attention(query, key, value, same_doc):
    length = query.shape[0]

    def split_heads(flat):
        return flat.reshape(length, -1, HEAD).transpose(1, 0, 2)
    heads = lax.map(jax.checkpoint(partial(head_attention, same_doc)), (split_heads(query), split_heads(key), split_heads(value)))
    return heads.transpose(1, 0, 2).reshape(length, -1)

def layer(inputs, params, same_doc, cosine, sine):
    query_weight, key_weight, value_weight, out_weight, query_bias, key_bias, value_bias, out_bias, first_gain, first_shift, up_weight, up_bias, down_weight, down_bias, second_gain, second_shift = params
    query = low(rotate(low_back(matmul(inputs, query_weight) + query_bias), cosine, sine))
    key = low(rotate(low_back(matmul(inputs, key_weight) + key_bias), cosine, sine))
    value = low(low_back(matmul(inputs, value_weight) + value_bias))
    attended = low(low_back(attention(query, key, value, same_doc)))
    branch = low_back(matmul(attended, out_weight) + out_bias)
    mid = layer_norm(inputs + branch, first_gain, first_shift)
    pre = low_back(matmul(low(mid), up_weight) + up_bias)
    active = low(jax.nn.gelu(pre, approximate=False))
    feed = low_back(matmul(active, down_weight) + down_bias)
    return layer_norm(mid + feed, second_gain, second_shift)

def reference(inputs, doc_lengths, query_weight, key_weight, value_weight, out_weight, query_bias, key_bias, value_bias, out_bias, first_gain, first_shift, up_weight, up_bias, down_weight, down_bias, second_gain, second_shift, cotangent):
    params = tuple((weight.astype(jnp.float32) for weight in (query_weight, key_weight, value_weight, out_weight, query_bias, key_bias, value_bias, out_bias, first_gain, first_shift, up_weight, up_bias, down_weight, down_bias, second_gain, second_shift)))

    def one_stream(totals, packed):
        rows, lengths, grad_out = packed
        same_doc, cosine, sine = document_tables(lengths)

        def forward(values, weights):
            return layer(values, weights, same_doc, cosine, sine)
        result, pullback = jax.vjp(forward, rows.astype(jnp.float32), params)
        grad_rows, grad_params = pullback(grad_out.astype(jnp.float32))
        totals = tuple((total + extra for total, extra in zip(totals, grad_params)))
        return (totals, (result.astype(jnp.bfloat16), grad_rows))
    zeros = tuple((jnp.zeros(weight.shape, jnp.float32) for weight in params))
    totals, (outputs, input_grads) = lax.scan(one_stream, zeros, (inputs, doc_lengths, cotangent))
    return (outputs, input_grads, totals[0], totals[1], totals[2], totals[3], totals[4], totals[5], totals[6], totals[7], totals[8], totals[9], totals[10], totals[11], totals[12], totals[13], totals[14], totals[15])
```

```python
import functools
import math

import jax
import jax.numpy as jnp
from jax import lax
from jax.experimental import pallas as pl
from jax.experimental.pallas import tpu as pltpu
from jax.sharding import PartitionSpec as P

HEADS = 12
HEAD = 64
EPSILON = 1e-05
AXES = ("group", "shard", "ctx")
BF = jnp.bfloat16
F32 = jnp.float32
MIB = 1024 * 1024
WORK = {"pack": 4, "tables": 4, "attention_forward": 18, "middle": 21, "attention_backward": 15, "down_grad": 5, "up_grad": 5,
        "qkv_grad": 4, "input_grad": 7}
ANY = pl.BlockSpec(memory_space=pl.ANY)
SMEM = pl.BlockSpec(memory_space=pltpu.SMEM)


def product(left, right):
    return jnp.dot(left, right, preferred_element_type=F32)


def inner_rows(left, right):
    return lax.dot_general(left, right, (((0,), (0,)), ((), ())), preferred_element_type=F32)


def times_transpose(left, right):
    return lax.dot_general(left, right, (((1,), (1,)), ((), ())), preferred_element_type=F32)


def column_sum(value):
    return jnp.sum(value.astype(F32), axis=0, keepdims=True)


def cut(value, start, size, axis):
    return lax.dynamic_slice_in_dim(value, start, size, axis=axis)


def run(kernel, name, outs, operands, modes=None, scratch=(), raw_outs=()):
    modes = modes or "s" * len(operands)
    staged = [i for i, m in enumerate(modes) if m not in ("r", "m")]
    parts = [modes[i] if isinstance(modes[i], tuple) else (0, operands[i].shape[0]) for i in staged]
    held = [i for i in range(len(outs)) if i not in raw_outs]
    n, k = len(operands), len(outs)

    def body(*refs):
        ins, results = list(refs[:n]), list(refs[n:n + k])
        rest = refs[n + k:]
        slots, rest = rest[:len(staged)], rest[len(staged):]
        buffers, rest = rest[:len(held)], rest[len(held):]
        in_sems, out_sems, rest = rest[0], rest[1], rest[2:]
        copies = []
        for at, i in enumerate(staged):
            source = ins[i].at[pl.ds(*parts[at])] if isinstance(modes[i], tuple) else ins[i]
            copies.append(pltpu.make_async_copy(source, slots[at], in_sems.at[at]))
            copies[-1].start()
            ins[i] = slots[at]
        sent = {}

        def emit(i):
            at = held.index(i)
            sent[i] = pltpu.make_async_copy(buffers[at], refs[n + i], out_sems.at[at])
            sent[i].start()

        for at, i in enumerate(held):
            results[i] = buffers[at]
        kernel(lambda: wait_all(copies), emit, *ins, *results, *rest)
        for i in held:
            if i not in sent:
                emit(i)
        wait_all(sent.values())

    return pl.pallas_call(
        body,
        out_shape=outs,
        in_specs=[SMEM if m == "m" else ANY for m in modes],
        out_specs=[ANY] * k,
        scratch_shapes=[pltpu.VMEM((rows, *operands[i].shape[1:]), operands[i].dtype) for i, (_, rows) in zip(staged, parts)]
        + [pltpu.VMEM(outs[i].shape, outs[i].dtype) for i in held]
        + [pltpu.SemaphoreType.DMA((max(len(staged), 1),)), pltpu.SemaphoreType.DMA((max(len(held), 1),))]
        + list(scratch),
        cost_estimate=pl.CostEstimate(flops=int(WORK[name] * 1.0 * 1e9), bytes_accessed=1, transcendentals=0),
        compiler_params=pltpu.CompilerParams(vmem_limit_bytes=62 * MIB),
        name=name,
    )(*operands)


def wait_all(copies):
    for c in copies:
        c.wait()


def shape(dims, dtype=BF):
    return jax.ShapeDtypeStruct(tuple(dims), dtype)


def position():
    s = lax.axis_index("shard")
    return lax.axis_index("group") & 1, s, lax.axis_index("ctx")


def pack_kernel(r, ready, emit, q_ref, k_ref, v_ref, o_ref, u_ref, qkv_send, qkv_ref, ou_ref, sems):
    half_g, _, _ = position()
    half = r // 2
    width = o_ref.shape[1]
    copies = []

    def copy(src, dst):
        copies.append(pltpu.make_async_copy(src, dst, sems.at[len(copies)]))
        copies[-1].start()

    mine = pl.ds(pl.multiple_of(half_g * half, half), half)
    for i, ref in enumerate((q_ref, k_ref, v_ref)):
        copy(ref.at[mine], qkv_send.at[pl.ds(i * half, half)])
    for h in range(2):
        rows = pl.ds(h * half, half)
        for i, ref in enumerate((q_ref, k_ref, v_ref)):
            copy(ref.at[rows], qkv_ref.at[h, pl.ds(i * half, half)])
    copy(o_ref, ou_ref.at[pl.ds(0, r)])
    for j in range(4):
        copy(u_ref.at[:, pl.ds(j * width, width)], ou_ref.at[pl.ds((1 + j) * r, r)])
    wait_all(copies[:3])
    emit(0)
    wait_all(copies[3:9])
    emit(1)
    wait_all(copies[9:])


class Loader:
    def __init__(self, sems):
        self.sems = sems
        self.used = 0

    def start(self, refs, r, targets):
        half_g, s, _ = position()
        if len(refs) == 4:
            copies = []
            for at, rows, target in targets:
                for i, ref in enumerate(refs):
                    start = pl.multiple_of((s ^ i) * rows, rows)
                    c = pltpu.make_async_copy(ref.at[pl.ds(at, rows)], target(pl.ds(start, rows)), self.sems.at[self.used])
                    self.used += 1
                    c.start()
                    copies.append(c)
            return copies
        own, near, first, second, near_first, near_second = refs
        pieces = [
            (own.at[0], s, 0),
            (own.at[1], s, 1),
            (near.at[0], s ^ 1, 0),
            (near.at[1], s ^ 1, 1),
            (first, s ^ 2, half_g),
            (second, s ^ 2, half_g ^ 1),
            (near_first, s ^ 3, half_g),
            (near_second, s ^ 3, half_g ^ 1),
        ]
        copies = []
        for at, rows, target in targets:
            for ref, shard, half in pieces:
                start = pl.multiple_of(shard * 2 * rows + half * rows, rows)
                c = pltpu.make_async_copy(ref.at[pl.ds(at, rows)], target(pl.ds(start, rows)), self.sems.at[self.used])
                self.used += 1
                c.start()
                copies.append(c)
        return copies


def tables_kernel(count, ready, emit, lengths_ref, cos_ref, sin_ref, dcol_ref, drow_ref):
    _, _, c = position()
    starts = []
    at = jnp.int32(0)
    for j in range(lengths_ref.shape[1]):
        starts.append(at)
        at = at + lengths_ref[0, j]

    def locate(place):
        number = jnp.zeros(place.shape, jnp.int32)
        first = jnp.zeros(place.shape, jnp.int32)
        for start in starts:
            past = start <= place
            number = number + jnp.where(past, 1, 0)
            first = jnp.maximum(first, jnp.where(past, start, 0))
        return number, first

    blocks = cos_ref.shape[0] // count
    lane = lax.broadcasted_iota(jnp.int32, (1, 128), 1)
    freqs = jnp.exp(((lane % HEAD) // 2).astype(F32) * (-2.0 / HEAD * math.log(10000.0)))
    sign = jnp.where(lane < HEAD, 1.0, -1.0)
    for m in range(blocks):
        base = (c ^ m) * count
        spot = base + lax.broadcasted_iota(jnp.int32, (count, 128), 0)
        number, first = locate(spot)
        dcol_ref[m * count:(m + 1) * count, :] = number[:, :1].astype(F32)
        angles = (spot - first).astype(F32) * freqs
        cos_ref[m * count:(m + 1) * count, :] = jnp.cos(angles)
        sin_ref[m * count:(m + 1) * count, :] = jnp.sin(angles) * sign
        across = base + lax.broadcasted_iota(jnp.int32, (1, count), 1)
        drow_ref[:, m * count:(m + 1) * count] = locate(across)[0].astype(F32)


def spread_of(rows, hpd, group):
    row = lax.broadcasted_iota(jnp.int32, (rows, 128 * hpd), 0) - group * (64 * hpd)
    lane = lax.broadcasted_iota(jnp.int32, (rows, 128 * hpd), 1)
    column = (lane // 128) * 64 + lane % 64
    odd = lane % 2
    swapped = lane % 128 >= 64
    partner = column + 1 - 2 * odd
    plain = jnp.where(swapped, 0.0, jnp.where(row == column, 1.0, 0.0))
    turned = jnp.where(swapped, jnp.where(row == partner, jnp.where(odd == 1, 1.0, -1.0), 0.0), 0.0)
    return (plain + turned).astype(BF)


def pick_of(rows, wide, group):
    row = lax.broadcasted_iota(jnp.int32, (rows, wide), 0)
    lane = lax.broadcasted_iota(jnp.int32, (rows, wide), 1)
    return jnp.where(row == lane + group * wide, 1.0, 0.0).astype(BF)


def forward_kernel(hpd, ctx, r, ready, emit, *refs):
    x_refs = refs[:ctx]
    piece_refs = refs[ctx:ctx + 6]
    small_refs = refs[ctx + 6:ctx + 10]
    cos_ref, sin_ref, dcol_ref, drow_ref = refs[ctx + 10:ctx + 14]
    att_refs = refs[ctx + 14:2 * ctx + 14]
    (q_ref, k_ref, v_ref, vec_ref, probs_out, probs_ref, w_ref, small_ref, wq_ref, wk_ref, wv_ref, att_ref, probs_sems,
     sems) = refs[2 * ctx + 14:]
    _, s, c = position()
    half = r // 2
    count, width = x_refs[0].shape
    length = count * ctx
    loader = Loader(sems)
    small = loader.start(small_refs, 16, [(0, 16, lambda rows: small_ref.at[rows])])
    copies = loader.start(piece_refs, r, [(i * half, half, lambda rows, i=i: w_ref.at[i, rows]) for i in range(3)])
    spread = spread_of(width, hpd, c)
    pick = pick_of(width, 64 * hpd, c)
    wait_all(small)
    per_row = width // r
    lines = []
    for i in range(9):
        parts = [
            small_ref[pl.ds(16 * p + 1 + i // per_row, 1), r * (i % per_row):r * (i % per_row) + r].astype(F32)
            for p in range(4)
        ]
        lines.append(jnp.concatenate(parts, axis=1))
    lines += [small_ref[pl.ds(16 * p, 1), :].astype(F32) for p in range(4)]
    lines.append(jnp.zeros((3, width), F32))
    vec = jnp.concatenate(lines, axis=0).astype(BF)
    vec_ref[...] = vec
    bq = product(vec, spread)[0:1]
    bk = product(vec, spread)[1:2]
    bv = product(vec, pick)[2:3]
    wait_all(copies)
    wq_ref[...] = product(w_ref[0], spread).astype(BF)
    wk_ref[...] = product(w_ref[1], spread).astype(BF)
    wv_ref[...] = product(w_ref[2], pick).astype(BF)
    ready()
    for m in range(ctx):
        rows = slice(m * count, (m + 1) * count)
        x = x_refs[m][...]
        for h in range(hpd):
            lanes = slice(128 * h, 128 * h + 128)
            for weight, bias, out in ((wq_ref, bq, q_ref), (wk_ref, bk, k_ref)):
                y = product(x, weight[:, lanes]) + bias[:, lanes]
                out[rows, lanes] = (y * cos_ref[rows, :] + pltpu.roll(y, 64, 1) * sin_ref[rows, :]).astype(BF)
        v_ref[rows, :] = (product(x, wv_ref[...]) + bv).astype(BF)

    once = 256

    def attend(step, carry):
        rows = pl.ds(pl.multiple_of(step * once, once), once)
        same = dcol_ref[rows, :] == drow_ref[...]
        for h in range(hpd):
            lanes = slice(128 * h, 128 * h + 128)
            scores = times_transpose(q_ref[rows, lanes], k_ref[:, lanes]) * (0.5 * HEAD ** (-0.5))
            scores = jnp.where(same, scores, -jnp.inf)
            peak = jnp.max(scores, axis=1, keepdims=True)
            expo = jnp.exp(scores - peak)
            total = jnp.sum(expo, axis=1, keepdims=True)
            probs = (expo * (1.0 / total)).astype(BF)
            probs_ref[h, rows, :] = probs
            att_ref[rows, 64 * h:64 * h + 64] = product(probs, v_ref[:, 64 * h:64 * h + 64]).astype(BF)
        probs_copy(step).start()
        return carry

    def probs_copy(step):
        rows = pl.ds(pl.multiple_of(step * once, once), once)
        return pltpu.make_async_copy(probs_ref.at[:, rows], probs_out.at[:, rows], probs_sems.at[step])

    for i in range(ctx, ctx + 4):
        emit(i)
    lax.fori_loop(0, length // once, attend, 0)
    for m in range(ctx):
        att_refs[m][...] = att_ref[m * count:(m + 1) * count, :]
        emit(m)
    for step in range(length // once):
        probs_copy(step).wait()


def backward_kernel(hpd, ctx, ready, emit, *refs):
    probs_in, q_ref, k_ref, v_ref, cos_ref, sin_ref = refs[:6]
    grad_refs = refs[6:6 + ctx]
    out_refs = refs[6 + ctx:6 + 2 * ctx]
    probs_ref, grad_ref, out_ref, gk_ref, gv_ref, probs_sems = refs[6 + 2 * ctx:]
    length = q_ref.shape[0]
    count = length // ctx
    once = 256
    factor = HEAD ** (-0.5)

    def probs_copy(step):
        rows = pl.ds(pl.multiple_of(step * once, once), once)
        return pltpu.make_async_copy(probs_in.at[:, rows], probs_ref.at[:, rows], probs_sems.at[step])

    for step in range(length // once):
        probs_copy(step).start()
    ready()
    for m in range(ctx):
        grad_ref[m * count:(m + 1) * count, :] = grad_refs[m][...]
    gk_ref[...] = jnp.zeros_like(gk_ref)
    gv_ref[...] = jnp.zeros_like(gv_ref)

    def step_of(step, carry):
        rows = pl.ds(pl.multiple_of(step * once, once), once)
        probs_copy(step).wait()
        for h in range(hpd):
            lanes = slice(128 * h, 128 * h + 128)
            narrow = slice(64 * h, 64 * h + 64)
            low = probs_ref[h, rows, :]
            probs = low.astype(F32)
            grad = grad_ref[rows, narrow]
            grad_probs = times_transpose(grad, v_ref[:, narrow])
            inner = jnp.sum(probs * grad_probs, axis=1, keepdims=True)
            grad_scores = (probs * (grad_probs - inner)).astype(BF)
            turned = product(grad_scores, k_ref[:, lanes]) * factor
            back = turned * cos_ref[rows, :] - pltpu.roll(turned, 64, 1) * sin_ref[rows, :]
            out_ref[rows, narrow] = back[:, :64].astype(BF)
            gk_ref[:, lanes] += inner_rows(grad_scores, q_ref[rows, lanes])
            gv_ref[:, narrow] += inner_rows(low, grad)
        return carry

    lax.fori_loop(0, length // once, step_of, 0)
    for h in range(hpd):
        turned = gk_ref[:, 128 * h:128 * h + 128] * factor
        back = turned * cos_ref[...] - pltpu.roll(turned, 64, 1) * sin_ref[...]
        out_ref[:, 64 * (hpd + h):64 * (hpd + h) + 64] = back[:, :64].astype(BF)
    out_ref[:, 128 * hpd:192 * hpd] = gv_ref[...].astype(BF)
    for m in range(ctx):
        out_refs[m][...] = out_ref[m * count:(m + 1) * count, :]


def normal(value):
    mean = jnp.mean(value, axis=-1, keepdims=True)
    centred = value - mean
    scale = lax.rsqrt(jnp.mean(centred * centred, axis=-1, keepdims=True) + EPSILON)
    return centred * scale, scale


def normal_back(grad, unit, scale, gain):
    inner = grad * gain
    return scale * (
        inner - jnp.mean(inner, axis=-1, keepdims=True) - unit * jnp.mean(inner * unit, axis=-1, keepdims=True)
    )


def error_function(x):
    x = jnp.clip(x, -4.0, 4.0)
    x2 = x * x
    top = jnp.float32(-2.72614225801306e-10)
    for a in (2.77068142495902e-08, -2.10102402082508e-06, -5.69250639462346e-05, -7.34990630326855e-04,
              -2.95459980854025e-03, -1.60960333262415e-02):
        top = top * x2 + a
    low = jnp.float32(-1.45660718464996e-05)
    for b in (-2.13374055278905e-04, -1.68282697438203e-03, -7.37332916720468e-03, -1.42647390514189e-02):
        low = low * x2 + b
    return x * top / low


def load_ou(loader, refs, r, w_out, w_up):
    targets = [(0, r, lambda rows: w_out.at[rows])]
    targets += [((1 + j) * r, r, lambda rows, j=j: w_up.at[j, rows]) for j in range(4)]
    return loader.start(refs, r, targets)


def load_down(loader, refs, r, w_down):
    return loader.start(refs, r, [(0, 4 * r, lambda rows: w_down.at[rows])])


def middle_kernel(ctx, r, ready, emit, *refs):
    att_refs = refs[:ctx]
    ou_refs, d_refs = refs[ctx:ctx + 4], refs[ctx + 4:ctx + 8]
    rows_ref, back_ref, vec_ref = refs[ctx + 8:ctx + 11]
    ga_refs = refs[ctx + 11:2 * ctx + 11]
    output_ref, first_ref, own_ref, near_ref, chip_ref, far_ref, gf_ref, cross_ref = refs[2 * ctx + 11:2 * ctx + 19]
    (w_out, w_up, w_down, act_ref, slope_ref, gp_ref, dw_ref, low_ref, mid_ref, unit_ref, feed_ref, bias_ref,
     sums_ref, sems) = refs[2 * ctx + 19:]
    half_g, s, c = position()
    core = s & 1
    loader = Loader(sems)
    first = load_ou(loader, ou_refs, r, w_out, w_up)
    second = load_down(loader, d_refs, r, w_down)
    wide = att_refs[0].shape[1]
    count, width = rows_ref.shape

    def vec(i):
        return vec_ref[i:i + 1, :].astype(F32)

    def place(m):
        return pl.ds(pl.multiple_of((c ^ m) * wide, wide), wide)

    def down_rows(j):
        return pl.ds(pl.multiple_of(j * 4 * r, 4 * r), 4 * r)

    if w_out.shape[0] > width:
        w_out[width:, :] = jnp.zeros((w_out.shape[0] - width, width), BF)
    ready()
    for j in range(4):
        bias_ref[j] = vec(9 + j)
    wait_all(first)
    total = rows_ref[...].astype(F32) + vec(3)
    for m in range(ctx):
        total = total + product(att_refs[m][...], w_out[place(m), :])
    unit, scale = normal(total)
    unit_ref[...] = unit
    mid = unit * vec(4) + vec(5)
    mid_ref[...] = mid
    low = mid.astype(BF)
    low_ref[...] = low
    parts = [low[:, i * r:(i + 1) * r] for i in range(4)]
    even = jnp.concatenate([parts[0], parts[2]], axis=1)
    odd = jnp.concatenate([parts[1], parts[3]], axis=1)
    mine = jnp.where(core == 0, even, odd)
    other = jnp.where(core == 0, odd, even)
    at, top = 4 * count, count // 2
    for ref, start, value in ((own_ref, at, mine), (near_ref, at, other), (cross_ref, 2 * count, other),
                              (cross_ref, 2 * count + top, mine)):
        ref[start:start + top, :2 * r] = value[:top]
        ref[start:start + top, 2 * r:] = value[top:]

    def up(j, carry):
        pre = product(low_ref[...], w_up[j]) + bias_ref[j]
        below = 0.5 + 0.5 * error_function(pre * (0.5 ** 0.5))
        slope = below + pre * jnp.exp(-0.5 * pre * pre) * (1.0 / math.sqrt(2.0 * math.pi))
        slope_ref[j] = slope.astype(BF)
        act_ref[j] = (pre * below).astype(BF)
        return carry

    lax.fori_loop(0, 4, up, 0)
    chip_ref[...] = act_ref[s ^ 2]
    emit(ctx + 4)
    far_ref[...] = act_ref[s ^ 3]
    emit(ctx + 5)
    own_ref[:count, :] = act_ref[s]
    near_ref[:count, :] = act_ref[s ^ 1]
    wait_all(second)
    feed_ref[...] = mid_ref[...] + vec(6)

    def down(j, carry):
        feed_ref[...] += product(act_ref[j], w_down[down_rows(j), :])
        return carry

    lax.fori_loop(0, 4, down, 0)
    unit_two, scale_two = normal(feed_ref[...])
    output_ref[...] = (unit_two * vec(7) + vec(8)).astype(BF)
    emit(ctx)
    back = back_ref[...].astype(F32)
    second_sums = [column_sum(back * unit_two), column_sum(back)]
    grad_second = normal_back(back, unit_two, scale_two, vec(7))
    feed_ref[...] = grad_second
    grad_feed = grad_second.astype(BF)
    gf_ref[...] = grad_feed
    emit(ctx + 6)
    own_ref[count:2 * count, :] = grad_feed
    near_ref[count:2 * count, :] = grad_feed

    def up_back(j, carry):
        grad_pre = (slope_ref[j].astype(F32) * times_transpose(gf_ref[...], w_down[down_rows(j), :])).astype(BF)
        gp_ref[j] = grad_pre
        sums_ref[j] = column_sum(grad_pre)
        return carry

    lax.fori_loop(0, 4, up_back, 0)
    for i in range(2):
        here = gp_ref[2 * half_g + i]
        own_ref[(2 + i) * count:(3 + i) * count, :] = here
        near_ref[(2 + i) * count:(3 + i) * count, :] = here
        cross_ref[i * count:(i + 1) * count, :] = gp_ref[2 * (half_g ^ 1) + i]
    emit(ctx + 7)

    def mid_back(j, carry):
        feed_ref[...] += times_transpose(gp_ref[j], w_up[j])
        return carry

    lax.fori_loop(0, 4, mid_back, 0)
    grad_mid = feed_ref[...]
    unit = unit_ref[...]
    grad_first = normal_back(grad_mid, unit, scale, vec(4))
    first_ref[...] = grad_first
    grad_branch = grad_first.astype(BF)
    for m in range(ctx):
        ga_refs[m][...] = times_transpose(grad_branch, w_out[place(m), :]).astype(BF)
        emit(m)
    for m in range(ctx):
        dw_ref[place(m), :] = inner_rows(att_refs[m][...], grad_branch)
    extra = jnp.concatenate(
        [column_sum(grad_branch), column_sum(grad_mid * unit), column_sum(grad_mid), *second_sums, column_sum(grad_feed)]
        + [sums_ref[j] for j in range(4)] + [jnp.zeros((6, width), F32)],
        axis=0,
    ).astype(BF)
    at = 4 * count + top
    for ref, which in ((own_ref, core), (near_ref, core ^ 1)):
        for x in range(2):
            part = dw_ref[pl.ds(pl.multiple_of((2 * x + which) * r, r), r), :]
            ref[at + x * r:at + (x + 1) * r, :] = part.astype(BF)
        ref[at + 2 * r:, :] = extra


def down_grad_kernel(r, ready, emit, a0, g0, a1, g1, a2, a3, g2, g3, okeep_ref, ocame_ref, keep_ref, send_ref, dw_ref):
    half_g, _, _ = position()
    ready()
    dw_ref[...] = inner_rows(a0[...], g0[...])
    for a, g in ((a1, g1), (a2, g2), (a3, g3)):
        dw_ref[...] += inner_rows(a[...], g[...])
    half = 2 * r
    keep_ref[:half, :] = dw_ref[pl.ds(pl.multiple_of(half_g * half, half), half), :].astype(BF)
    send_ref[:half, :] = dw_ref[pl.ds(pl.multiple_of((half_g ^ 1) * half, half), half), :].astype(BF)
    low = okeep_ref[0:r // 2, :].astype(F32) + ocame_ref[0:r // 2, :].astype(F32)
    high = okeep_ref[r // 2:r, :].astype(F32) + ocame_ref[r // 2:r, :].astype(F32)
    extra = (okeep_ref[r:, :].astype(F32) + ocame_ref[r:, :].astype(F32)).astype(BF)
    keep_ref[half:half + r // 2, :] = jnp.where(half_g == 0, low, high).astype(BF)
    send_ref[half:half + r // 2, :] = jnp.where(half_g == 0, high, low).astype(BF)
    keep_ref[half + r // 2:, :] = extra
    send_ref[half + r // 2:, :] = extra


def up_grad_kernel(r, ready, emit, p0, m0, p1, m1, p2, m2, p3, m3, keep_ref, send_ref, dw_ref):
    _, s, _ = position()
    chip = s >> 1
    ready()
    top = m0.shape[0]
    for j in range(2):
        for i, (m, p) in enumerate(((m0, p0), (m1, p1), (m2, p2), (m3, p3))):
            at = 2 * j * top
            part = inner_rows(m[:, :2 * r], p[at:at + top]) + inner_rows(m[:, 2 * r:], p[at + top:at + 2 * top])
            dw_ref[j] = part if i == 0 else dw_ref[j] + part
        keep_ref[j * r:(j + 1) * r, :] = dw_ref[j, pl.ds(pl.multiple_of(chip * r, r), r), :].astype(BF)
        send_ref[j * r:(j + 1) * r, :] = dw_ref[j, pl.ds(pl.multiple_of((chip ^ 1) * r, r), r), :].astype(BF)


def qkv_grad_kernel(ctx, r, ready, emit, *refs):
    x_refs, g_refs = refs[:ctx], refs[ctx:2 * ctx]
    keep_ref, send_ref, dw_ref = refs[2 * ctx:]
    _, s, _ = position()
    core = s & 1
    ready()
    dw_ref[...] = inner_rows(x_refs[0][...], g_refs[0][...])
    bias = column_sum(g_refs[0][...])
    for m in range(1, ctx):
        dw_ref[...] += inner_rows(x_refs[m][...], g_refs[m][...])
        bias = bias + column_sum(g_refs[m][...])
    extra = jnp.concatenate([bias, jnp.zeros((15, bias.shape[1]), F32)], axis=0).astype(BF)
    for x in range(2):
        keep_ref[x * r:(x + 1) * r, :] = dw_ref[pl.ds(pl.multiple_of((2 * x + core) * r, r), r), :].astype(BF)
        send_ref[x * r:(x + 1) * r, :] = dw_ref[pl.ds(pl.multiple_of((2 * x + (core ^ 1)) * r, r), r), :].astype(BF)
    keep_ref[2 * r:, :] = extra
    send_ref[2 * r:, :] = extra


def input_grad_kernel(ctx, r, ready, emit, *refs):
    g_refs = refs[:ctx]
    piece_refs = refs[ctx:ctx + 6]
    first_ref, out_ref, w_ref, sems = refs[ctx + 6:]
    _, _, c = position()
    half = r // 2
    copies = Loader(sems).start(piece_refs, r, [(i * half, half, lambda rows, i=i: w_ref.at[i, rows]) for i in range(3)])
    count, width = first_ref.shape
    wide = g_refs[0].shape[1] // 3
    places = []
    for m in range(ctx):
        row = lax.broadcasted_iota(jnp.int32, (wide, width), 0)
        lane = lax.broadcasted_iota(jnp.int32, (wide, width), 1)
        places.append(jnp.where(lane == row + (c ^ m) * wide, 1.0, 0.0).astype(BF))
    ready()
    full = []
    for i in range(3):
        total = product(g_refs[0][:, i * wide:(i + 1) * wide], places[0])
        for m in range(1, ctx):
            total = total + product(g_refs[m][:, i * wide:(i + 1) * wide], places[m])
        full.append(total.astype(BF))
    wait_all(copies)
    total = first_ref[...]
    for i in range(3):
        total = total + times_transpose(full[i], w_ref[i])
    out_ref[...] = total


def shards(
    inputs,
    doc_lengths,
    query_weight,
    key_weight,
    value_weight,
    out_weight,
    query_bias,
    key_bias,
    value_bias,
    out_bias,
    first_gain,
    first_shift,
    up_weight,
    up_bias,
    down_weight,
    down_bias,
    second_gain,
    second_shift,
    cotangent,
):
    groups, shard_count, ctx = (lax.axis_size(name) for name in AXES)
    here_g, here_s, here_c = (lax.axis_index(name) for name in AXES)
    chip = here_s >> 1
    half_g = here_g & 1
    ctx_bits = ctx.bit_length() - 1
    group_bits = groups.bit_length() - 1

    def move(value, dg=0, ds=0, dc=0):
        pairs = []
        for g in range(groups):
            for s in range(shard_count):
                for c in range(ctx):
                    there = ((g ^ dg) * shard_count + (s ^ ds)) * ctx + (c ^ dc)
                    pairs.append(((g * shard_count + s) * ctx + c, there))
        return lax.ppermute(value, AXES, pairs)

    def in_order(blocks, index):
        bit = 1
        while bit < len(blocks):
            swap = (index & bit) != 0
            blocks = [jnp.where(swap, blocks[m ^ bit], blocks[m]) for m in range(len(blocks))]
            bit *= 2
        return blocks

    rows = inputs[0]
    count, width = rows.shape
    length = count * ctx
    hpd = -(-HEADS // ctx)
    slots = hpd * ctx
    wide = 64 * hpd
    r = query_weight.shape[0]
    half = r // 2

    def after(value, *others):
        return lax.optimization_barrier((value, others))[0]

    blocks = {0: rows}
    for b in reversed(range(ctx_bits)):
        bit = 1 << b
        blocks.update({m ^ bit: move(v, dc=bit) for m, v in list(blocks.items())})
    xs = [blocks[m] for m in range(ctx)]
    qkv_send, qkv_own, ou_own = run(
        functools.partial(pack_kernel, r),
        "pack",
        [shape((3 * half, width)), shape((2, 3 * half, width)), shape((5 * r, width))],
        (query_weight, key_weight, value_weight, out_weight, up_weight),
        "rrrrr",
        [pltpu.SemaphoreType.DMA((14,))],
    )

    def spread_out(own, first):
        second = move(first, dg=1)
        return (own, move(own, ds=1), first, second, move(first, ds=1), move(second, ds=1))

    qkv_first = move(qkv_send, ds=2)
    qkv = spread_out(qkv_own, qkv_first)
    small = jnp.concatenate(
        [after(up_bias, qkv_send), query_bias, key_bias, value_bias, out_bias, first_gain, first_shift, down_bias,
         second_gain, second_shift]
    )
    small = jnp.pad(small, (0, 16 * width - small.shape[0])).reshape(16, width)
    small_far = move(small, ds=2)
    small = (small, move(small, ds=1), small_far, move(small_far, ds=1))

    d_far = move(after(down_weight, qkv_first, small_far), ds=2)
    ou_far = move(after(ou_own, d_far, xs), ds=2)

    cosine, sine, dcol, drow = run(
        functools.partial(tables_kernel, count),
        "tables",
        [shape((length, 128), F32), shape((length, 128), F32), shape((length, 1), F32), shape((1, length), F32)],
        (after(doc_lengths, small_far),),
        "m",
    )

    steps = length // 256
    outs = run(
        functools.partial(forward_kernel, hpd, ctx, r),
        "attention_forward",
        [shape((count, wide))] * ctx
        + [shape((length, 128 * hpd)), shape((length, 128 * hpd)), shape((length, wide)), shape((16, width)),
           shape((hpd, length, length))],
        (*xs, *qkv, *small, cosine, sine, dcol, drow),
        "s" * ctx + "r" * 10 + "ssss",
        [pltpu.VMEM((hpd, length, length), BF), pltpu.VMEM((3, width, width), BF), pltpu.VMEM((64, width), BF),
         pltpu.VMEM((width, 128 * hpd), BF), pltpu.VMEM((width, 128 * hpd), BF), pltpu.VMEM((width, wide), BF),
         pltpu.VMEM((length, wide), BF), pltpu.SemaphoreType.DMA((steps,)), pltpu.SemaphoreType.DMA((28,))],
        raw_outs=(ctx + 4,),
    )
    att, (q_turned, k_turned, v_low, vec, probs) = outs[:ctx], outs[ctx:]

    def exchange_ctx(pieces):
        return [pieces[0]] + [move(pieces[m], dc=m) for m in range(1, ctx)]

    att = exchange_ctx(att)
    down = (down_weight, move(down_weight, ds=1), d_far, move(after(d_far, att), ds=1))
    ou = (ou_own, move(ou_own, ds=1), ou_far, move(after(ou_far, att), ds=1))
    tile = (count, width)
    packed = 4 * count + count // 2 + 2 * r + 16
    outs = run(
        functools.partial(middle_kernel, ctx, r),
        "middle",
        [shape((count, wide))] * ctx
        + [shape(tile), shape(tile, F32), shape((packed, width)), shape((packed, width)), shape(tile), shape(tile), shape(tile),
           shape((3 * count, width))],
        (*att, *ou, *down, rows, cotangent[0], vec),
        "s" * ctx + "r" * 8 + "sss",
        [pltpu.VMEM((max(slots * HEAD, width), width), BF), pltpu.VMEM((4, width, width), BF), pltpu.VMEM((4 * width, width), BF)]
        + [pltpu.VMEM((4, *tile), BF)] * 3
        + [pltpu.VMEM((max(slots * HEAD, width), width), F32), pltpu.VMEM(tile, BF)]
        + [pltpu.VMEM(tile, F32)] * 3 + [pltpu.VMEM((4, 1, width), F32)] * 2 + [pltpu.SemaphoreType.DMA((28,))],
    )
    grad_att, (output, grad_first, own, near_send, chip_send, far_send, grad_feed, cross_send) = outs[:ctx], outs[ctx:]

    def add(one, other):
        return (one.astype(F32) + other.astype(F32)).astype(BF)

    def ordered_pair(mine_part, other_part, bit_value, axis):
        low = jnp.where(bit_value == 0, mine_part, other_part)
        high = jnp.where(bit_value == 0, other_part, mine_part)
        return jnp.concatenate([low, high], axis=axis)

    def split(total, sizes, bit_value):
        keep, send = [], []
        at = 0
        for size in sizes:
            part = total[at:at + size]
            at += size
            keep.append(cut(part, bit_value * (size // 2), size // 2, 0))
            send.append(cut(part, (1 - bit_value) * (size // 2), size // 2, 0))
        rest = [total[at:]] if at < total.shape[0] else []
        return jnp.concatenate(keep + rest, axis=0), jnp.concatenate(send + rest, axis=0)

    def halve(total, sizes, bit_value, **how):
        keep, send = split(total, sizes, bit_value)
        return add(keep, move(send, **how)), [size // 2 for size in sizes]

    def double(total, sizes, bit_value, **how):
        came = move(total, **how)
        at, out = 0, []
        for size in sizes:
            out.append(ordered_pair(total[at:at + size], came[at:at + size], bit_value, 0))
            at += size
        return jnp.concatenate(out, axis=0), [2 * size for size in sizes]

    def reduce(total, sizes, steps):
        for bit_value, how in steps:
            total, sizes = halve(total, sizes, bit_value, **how)
        return total[:sum(sizes)], sizes, total[sum(sizes):]

    def gather(total, sizes, steps):
        for bit_value, how in reversed(steps):
            total, sizes = double(total, sizes, bit_value, **how)
        return total, sizes

    reduce_steps = [((here_g >> b) & 1, dict(dg=1 << b)) for b in range(1, group_bits)]
    reduce_steps += [((here_c >> b) & 1, dict(dc=1 << b)) for b in range(ctx_bits)]

    grad_att = exchange_ctx(grad_att)
    near = move(near_send, ds=1)
    chip_act = move(chip_send, ds=2)
    far_act = move(far_send, ds=3)
    chip_feed = move(grad_feed, ds=2)
    cross = move(cross_send, dg=1)
    mid_at = 4 * count
    o_at = mid_at + count // 2
    o_mid = add(own[o_at:], near[o_at:])
    o_keep, o_send = split(o_mid, [2 * r], chip)
    o_came = move(o_send, ds=2)

    grads = run(
        functools.partial(backward_kernel, hpd, ctx),
        "attention_backward",
        [shape((count, 3 * wide))] * ctx,
        (probs, q_turned, k_turned, v_low, cosine, after(sine, o_send), *grad_att),
        "r" + "s" * (5 + ctx),
        [pltpu.VMEM((hpd, length, length), BF), pltpu.VMEM((length, wide), BF), pltpu.VMEM((length, 3 * wide), BF),
         pltpu.VMEM((length, 128 * hpd), F32), pltpu.VMEM((length, wide), F32), pltpu.SemaphoreType.DMA((steps,))],
    )
    received = exchange_ctx(grads)
    far_feed = move(after(chip_feed, grads, chip_act, far_act, o_came), ds=1)
    cross_near = move(after(cross, grads, chip_act, far_act, o_came), ds=1)

    d_keep, d_send = run(
        functools.partial(down_grad_kernel, r),
        "down_grad",
        [shape((2 * r + half + 16, width))] * 2,
        (own, own, near, near, chip_act, far_act, chip_feed, far_feed, o_keep, after(o_came, grads)),
        [(0, count), (count, count)] * 2 + ["s"] * 6,
        scratch=[pltpu.VMEM((4 * r, width), F32)],
    )
    d_came = move(d_send, dg=1)

    u_keep, u_send = run(
        functools.partial(up_grad_kernel, r),
        "up_grad",
        [shape((2 * r, width))] * 2,
        (after(own, d_keep), own, near, near, cross, cross, cross_near, cross_near),
        [(2 * count, 2 * count), (mid_at, count // 2)] * 2
        + [(0, 2 * count), (2 * count + count // 2, count // 2), (0, 2 * count), (2 * count, count // 2)],
        scratch=[pltpu.VMEM((2, 2 * r, width), F32)],
    )
    u_came = move(u_send, ds=2)

    q_keep, q_send = run(
        functools.partial(qkv_grad_kernel, ctx, r),
        "qkv_grad",
        [shape((2 * r + 16, 3 * wide))] * 2,
        (*xs, after(grads[0], u_keep), *grads[1:]),
        scratch=[pltpu.VMEM((width, 3 * wide), F32)],
    )
    total_q = add(q_keep, move(q_send, ds=1))
    total_q, _ = halve(total_q, [2 * r], chip, ds=2)
    total_d = add(d_keep, d_came)
    total_u = add(u_keep, u_came)

    (input_grad,) = run(
        functools.partial(input_grad_kernel, ctx, r),
        "input_grad",
        [shape(tile, F32)],
        (*received, *qkv, after(grad_first, total_q)),
        "s" * ctx + "r" * 6 + "s",
        [pltpu.VMEM((3, width, width), BF), pltpu.SemaphoreType.DMA((24,))],
    )

    total = jnp.concatenate([total_d[:2 * r + half], after(total_u, received), total_d[2 * r + half:]], axis=0)
    total, sizes, extra = reduce(total, [2 * r, half, 2 * r], reduce_steps)
    total, sizes = gather(total, sizes, reduce_steps)
    total, sizes = double(total, sizes, half_g, dg=1)
    down_sum, out_sum = total[:4 * r].astype(F32), total[4 * r:5 * r].astype(F32)
    up_sum = jnp.concatenate([total[i * r:(i + 1) * r] for i in range(5, 9)], axis=1).astype(F32)

    total = total_q
    for b in range(group_bits):
        total = add(total, move(total, dg=1 << b))
    gathered = {0: total}
    for b in reversed(range(ctx_bits)):
        bit = 1 << b
        gathered.update({m ^ bit: move(v, dc=bit) for m, v in list(gathered.items())})
    gathered = in_order([gathered[m] for m in range(ctx)], here_c)
    extra_mine = cut(extra.astype(F32), here_s * r, r, 1)

    qkv_sums = []
    qkv_bias_sums = []
    for i in range(3):
        whole = jnp.concatenate([g[:r + 1, i * wide:(i + 1) * wide] for g in gathered], axis=1)[:, :width]
        qkv_sums.append(whole[:r].astype(F32))
        qkv_bias_sums.append(cut(whole[r].astype(F32), here_s * r, r, 0))

    return (
        output[None],
        input_grad[None],
        qkv_sums[0],
        qkv_sums[1],
        qkv_sums[2],
        out_sum,
        qkv_bias_sums[0],
        qkv_bias_sums[1],
        qkv_bias_sums[2],
        extra_mine[0],
        extra_mine[1],
        extra_mine[2],
        up_sum,
        lax.dynamic_index_in_dim(extra, 6 + here_s, 0, keepdims=False).astype(F32),
        down_sum,
        extra_mine[5],
        extra_mine[3],
        extra_mine[4],
    )


def solution(mesh):
    vector, matrix, tokens = P("shard"), P("shard", None), P(("group", "shard"), "ctx", None)
    weights = (matrix,) * 4 + (vector,) * 6 + (matrix, vector, matrix) + (vector,) * 3
    in_specs = (tokens, P(("group", "shard"), None)) + weights + (tokens,)
    out_specs = (tokens, tokens) + weights
    return jax.shard_map(shards, mesh=mesh, in_specs=in_specs, out_specs=out_specs, check_vma=False)
```

```python
import functools
import math

import jax
import jax.numpy as jnp
from jax import lax
from jax.experimental import pallas as pl
from jax.experimental.pallas import tpu as pltpu
from jax.sharding import PartitionSpec as P

HEADS = 12
HEAD = 64
EPSILON = 1e-05
AXES = ("group", "shard", "ctx")
BF = jnp.bfloat16
F32 = jnp.float32
MIB = 1024 * 1024
WORK = {"pack": 4, "tables": 4, "attention_forward": 18, "middle": 21, "attention_backward": 15, "down_grad": 5, "up_grad": 5,
        "qkv_grad": 4, "input_grad": 30}
ANY = pl.BlockSpec(memory_space=pl.ANY)
SMEM = pl.BlockSpec(memory_space=pltpu.SMEM)


def product(left, right):
    return jnp.dot(left, right, preferred_element_type=F32)


def inner_rows(left, right):
    return lax.dot_general(left, right, (((0,), (0,)), ((), ())), preferred_element_type=F32)


def times_transpose(left, right):
    return lax.dot_general(left, right, (((1,), (1,)), ((), ())), preferred_element_type=F32)


def column_sum(value):
    return jnp.sum(value.astype(F32), axis=0, keepdims=True)


def cut(value, start, size, axis):
    return lax.dynamic_slice_in_dim(value, start, size, axis=axis)


def run(kernel, name, outs, operands, modes=None, scratch=(), raw_outs=()):
    modes = modes or "s" * len(operands)
    staged = [i for i, m in enumerate(modes) if m not in ("r", "m")]
    parts = [modes[i] if isinstance(modes[i], tuple) else (0, operands[i].shape[0]) for i in staged]
    held = [i for i in range(len(outs)) if i not in raw_outs]
    n, k = len(operands), len(outs)

    def body(*refs):
        ins, results = list(refs[:n]), list(refs[n:n + k])
        rest = refs[n + k:]
        slots, rest = rest[:len(staged)], rest[len(staged):]
        buffers, rest = rest[:len(held)], rest[len(held):]
        in_sems, out_sems, rest = rest[0], rest[1], rest[2:]
        copies = []
        for at, i in enumerate(staged):
            source = ins[i].at[pl.ds(*parts[at])] if isinstance(modes[i], tuple) else ins[i]
            copies.append(pltpu.make_async_copy(source, slots[at], in_sems.at[at]))
            copies[-1].start()
            ins[i] = slots[at]
        sent = {}

        def emit(i):
            at = held.index(i)
            sent[i] = pltpu.make_async_copy(buffers[at], refs[n + i], out_sems.at[at])
            sent[i].start()

        for at, i in enumerate(held):
            results[i] = buffers[at]
        kernel(lambda: wait_all(copies), emit, *ins, *results, *rest)
        for i in held:
            if i not in sent:
                emit(i)
        wait_all(sent.values())

    return pl.pallas_call(
        body,
        out_shape=outs,
        in_specs=[SMEM if m == "m" else ANY for m in modes],
        out_specs=[ANY] * k,
        scratch_shapes=[pltpu.VMEM((rows, *operands[i].shape[1:]), operands[i].dtype) for i, (_, rows) in zip(staged, parts)]
        + [pltpu.VMEM(outs[i].shape, outs[i].dtype) for i in held]
        + [pltpu.SemaphoreType.DMA((max(len(staged), 1),)), pltpu.SemaphoreType.DMA((max(len(held), 1),))]
        + list(scratch),
        cost_estimate=pl.CostEstimate(flops=int(WORK[name] * 1.0 * 1e9), bytes_accessed=1, transcendentals=0),
        compiler_params=pltpu.CompilerParams(vmem_limit_bytes=62 * MIB),
        name=name,
    )(*operands)


def wait_all(copies):
    for c in copies:
        c.wait()


def shape(dims, dtype=BF):
    return jax.ShapeDtypeStruct(tuple(dims), dtype)


def position():
    s = lax.axis_index("shard")
    return lax.axis_index("group") & 1, s, lax.axis_index("ctx")


def pack_kernel(r, ready, emit, q_ref, k_ref, v_ref, o_ref, u_ref, qkv_send, qkv_ref, ou_ref, sems):
    half_g, _, _ = position()
    half = r // 2
    width = o_ref.shape[1]
    copies = []

    def copy(src, dst):
        copies.append(pltpu.make_async_copy(src, dst, sems.at[len(copies)]))
        copies[-1].start()

    mine = pl.ds(pl.multiple_of(half_g * half, half), half)
    for i, ref in enumerate((q_ref, k_ref, v_ref)):
        copy(ref.at[mine], qkv_send.at[pl.ds(i * half, half)])
    for h in range(2):
        rows = pl.ds(h * half, half)
        for i, ref in enumerate((q_ref, k_ref, v_ref)):
            copy(ref.at[rows], qkv_ref.at[h, pl.ds(i * half, half)])
    copy(o_ref, ou_ref.at[pl.ds(0, r)])
    for j in range(4):
        copy(u_ref.at[:, pl.ds(j * width, width)], ou_ref.at[pl.ds((1 + j) * r, r)])
    wait_all(copies[:3])
    emit(0)
    wait_all(copies[3:9])
    emit(1)
    wait_all(copies[9:])


class Loader:
    def __init__(self, sems):
        self.sems = sems
        self.used = 0

    def start(self, refs, r, targets):
        half_g, s, _ = position()
        if len(refs) == 4:
            copies = []
            for at, rows, target in targets:
                for i, ref in enumerate(refs):
                    start = pl.multiple_of((s ^ i) * rows, rows)
                    c = pltpu.make_async_copy(ref.at[pl.ds(at, rows)], target(pl.ds(start, rows)), self.sems.at[self.used])
                    self.used += 1
                    c.start()
                    copies.append(c)
            return copies
        own, near, first, second, near_first, near_second = refs
        pieces = [
            (own.at[0], s, 0),
            (own.at[1], s, 1),
            (near.at[0], s ^ 1, 0),
            (near.at[1], s ^ 1, 1),
            (first, s ^ 2, half_g),
            (second, s ^ 2, half_g ^ 1),
            (near_first, s ^ 3, half_g),
            (near_second, s ^ 3, half_g ^ 1),
        ]
        copies = []
        for at, rows, target in targets:
            for ref, shard, half in pieces:
                start = pl.multiple_of(shard * 2 * rows + half * rows, rows)
                c = pltpu.make_async_copy(ref.at[pl.ds(at, rows)], target(pl.ds(start, rows)), self.sems.at[self.used])
                self.used += 1
                c.start()
                copies.append(c)
        return copies


def tables_kernel(count, ready, emit, lengths_ref, cos_ref, sin_ref, dcol_ref, drow_ref):
    _, _, c = position()
    starts = []
    at = jnp.int32(0)
    for j in range(lengths_ref.shape[1]):
        starts.append(at)
        at = at + lengths_ref[0, j]

    def locate(place):
        number = jnp.zeros(place.shape, jnp.int32)
        first = jnp.zeros(place.shape, jnp.int32)
        for start in starts:
            past = start <= place
            number = number + jnp.where(past, 1, 0)
            first = jnp.maximum(first, jnp.where(past, start, 0))
        return number, first

    blocks = cos_ref.shape[0] // count
    lane = lax.broadcasted_iota(jnp.int32, (1, 128), 1)
    freqs = jnp.exp(((lane % HEAD) // 2).astype(F32) * (-2.0 / HEAD * math.log(10000.0)))
    sign = jnp.where(lane < HEAD, 1.0, -1.0)
    for m in range(blocks):
        base = (c ^ m) * count
        spot = base + lax.broadcasted_iota(jnp.int32, (count, 128), 0)
        number, first = locate(spot)
        dcol_ref[m * count:(m + 1) * count, :] = number[:, :1].astype(F32)
        angles = (spot - first).astype(F32) * freqs
        cos_ref[m * count:(m + 1) * count, :] = jnp.cos(angles)
        sin_ref[m * count:(m + 1) * count, :] = jnp.sin(angles) * sign
        across = base + lax.broadcasted_iota(jnp.int32, (1, count), 1)
        drow_ref[:, m * count:(m + 1) * count] = locate(across)[0].astype(F32)


def spread_of(rows, hpd, group):
    row = lax.broadcasted_iota(jnp.int32, (rows, 128 * hpd), 0) - group * (64 * hpd)
    lane = lax.broadcasted_iota(jnp.int32, (rows, 128 * hpd), 1)
    column = (lane // 128) * 64 + lane % 64
    odd = lane % 2
    swapped = lane % 128 >= 64
    partner = column + 1 - 2 * odd
    plain = jnp.where(swapped, 0.0, jnp.where(row == column, 1.0, 0.0))
    turned = jnp.where(swapped, jnp.where(row == partner, jnp.where(odd == 1, 1.0, -1.0), 0.0), 0.0)
    return (plain + turned).astype(BF)


def pick_of(rows, wide, group):
    row = lax.broadcasted_iota(jnp.int32, (rows, wide), 0)
    lane = lax.broadcasted_iota(jnp.int32, (rows, wide), 1)
    return jnp.where(row == lane + group * wide, 1.0, 0.0).astype(BF)


def forward_kernel(hpd, ctx, r, ready, emit, *refs):
    x_refs = refs[:ctx]
    piece_refs = refs[ctx:ctx + 6]
    small_refs = refs[ctx + 6:ctx + 10]
    cos_ref, sin_ref, dcol_ref, drow_ref = refs[ctx + 10:ctx + 14]
    att_refs = refs[ctx + 14:2 * ctx + 14]
    (q_ref, k_ref, v_ref, vec_ref, probs_out, probs_ref, w_ref, small_ref, wq_ref, wk_ref, wv_ref, att_ref, probs_sems,
     sems) = refs[2 * ctx + 14:]
    _, s, c = position()
    half = r // 2
    count, width = x_refs[0].shape
    length = count * ctx
    loader = Loader(sems)
    small = loader.start(small_refs, 16, [(0, 16, lambda rows: small_ref.at[rows])])
    copies = loader.start(piece_refs, r, [(i * half, half, lambda rows, i=i: w_ref.at[i, rows]) for i in range(3)])
    spread = spread_of(width, hpd, c)
    pick = pick_of(width, 64 * hpd, c)
    wait_all(small)
    per_row = width // r
    lines = []
    for i in range(9):
        parts = [
            small_ref[pl.ds(16 * p + 1 + i // per_row, 1), r * (i % per_row):r * (i % per_row) + r].astype(F32)
            for p in range(4)
        ]
        lines.append(jnp.concatenate(parts, axis=1))
    lines += [small_ref[pl.ds(16 * p, 1), :].astype(F32) for p in range(4)]
    lines.append(jnp.zeros((3, width), F32))
    vec = jnp.concatenate(lines, axis=0).astype(BF)
    vec_ref[...] = vec
    bq = product(vec, spread)[0:1]
    bk = product(vec, spread)[1:2]
    bv = product(vec, pick)[2:3]
    wait_all(copies)
    wq_ref[...] = product(w_ref[0], spread).astype(BF)
    wk_ref[...] = product(w_ref[1], spread).astype(BF)
    wv_ref[...] = product(w_ref[2], pick).astype(BF)
    ready()
    for m in range(ctx):
        rows = slice(m * count, (m + 1) * count)
        x = x_refs[m][...]
        for h in range(hpd):
            lanes = slice(128 * h, 128 * h + 128)
            for weight, bias, out in ((wq_ref, bq, q_ref), (wk_ref, bk, k_ref)):
                y = product(x, weight[:, lanes]) + bias[:, lanes]
                out[rows, lanes] = (y * cos_ref[rows, :] + pltpu.roll(y, 64, 1) * sin_ref[rows, :]).astype(BF)
        v_ref[rows, :] = (product(x, wv_ref[...]) + bv).astype(BF)

    once = 256

    def attend(step, carry):
        rows = pl.ds(pl.multiple_of(step * once, once), once)
        same = dcol_ref[rows, :] == drow_ref[...]
        for h in range(hpd):
            lanes = slice(128 * h, 128 * h + 128)
            scores = times_transpose(q_ref[rows, lanes], k_ref[:, lanes]) * (0.5 * HEAD ** (-0.5))
            scores = jnp.where(same, scores, -jnp.inf)
            peak = jnp.max(scores, axis=1, keepdims=True)
            expo = jnp.exp(scores - peak)
            total = jnp.sum(expo, axis=1, keepdims=True)
            probs = (expo * (1.0 / total)).astype(BF)
            probs_ref[h, rows, :] = probs
            att_ref[rows, 64 * h:64 * h + 64] = product(probs, v_ref[:, 64 * h:64 * h + 64]).astype(BF)
        probs_copy(step).start()
        return carry

    def probs_copy(step):
        rows = pl.ds(pl.multiple_of(step * once, once), once)
        return pltpu.make_async_copy(probs_ref.at[:, rows], probs_out.at[:, rows], probs_sems.at[step])

    for i in range(ctx, ctx + 4):
        emit(i)
    lax.fori_loop(0, length // once, attend, 0)
    for m in range(ctx):
        att_refs[m][...] = att_ref[m * count:(m + 1) * count, :]
        emit(m)
    for step in range(length // once):
        probs_copy(step).wait()


def backward_kernel(hpd, ctx, ready, emit, *refs):
    probs_in, q_ref, k_ref, v_ref, cos_ref, sin_ref = refs[:6]
    grad_refs = refs[6:6 + ctx]
    out_refs = refs[6 + ctx:6 + 2 * ctx]
    probs_ref, grad_ref, out_ref, gk_ref, gv_ref, probs_sems = refs[6 + 2 * ctx:]
    length = q_ref.shape[0]
    count = length // ctx
    once = 256
    factor = HEAD ** (-0.5)

    def probs_copy(step):
        rows = pl.ds(pl.multiple_of(step * once, once), once)
        return pltpu.make_async_copy(probs_in.at[:, rows], probs_ref.at[:, rows], probs_sems.at[step])

    for step in range(length // once):
        probs_copy(step).start()
    ready()
    for m in range(ctx):
        grad_ref[m * count:(m + 1) * count, :] = grad_refs[m][...]
    gk_ref[...] = jnp.zeros_like(gk_ref)
    gv_ref[...] = jnp.zeros_like(gv_ref)

    def step_of(step, carry):
        rows = pl.ds(pl.multiple_of(step * once, once), once)
        probs_copy(step).wait()
        for h in range(hpd):
            lanes = slice(128 * h, 128 * h + 128)
            narrow = slice(64 * h, 64 * h + 64)
            low = probs_ref[h, rows, :]
            probs = low.astype(F32)
            grad = grad_ref[rows, narrow]
            grad_probs = times_transpose(grad, v_ref[:, narrow])
            inner = jnp.sum(probs * grad_probs, axis=1, keepdims=True)
            grad_scores = (probs * (grad_probs - inner)).astype(BF)
            turned = product(grad_scores, k_ref[:, lanes]) * factor
            back = turned * cos_ref[rows, :] - pltpu.roll(turned, 64, 1) * sin_ref[rows, :]
            out_ref[rows, narrow] = back[:, :64].astype(BF)
            gk_ref[:, lanes] += inner_rows(grad_scores, q_ref[rows, lanes])
            gv_ref[:, narrow] += inner_rows(low, grad)
        return carry

    lax.fori_loop(0, length // once, step_of, 0)
    for h in range(hpd):
        turned = gk_ref[:, 128 * h:128 * h + 128] * factor
        back = turned * cos_ref[...] - pltpu.roll(turned, 64, 1) * sin_ref[...]
        out_ref[:, 64 * (hpd + h):64 * (hpd + h) + 64] = back[:, :64].astype(BF)
    out_ref[:, 128 * hpd:192 * hpd] = gv_ref[...].astype(BF)
    for m in range(ctx):
        out_refs[m][...] = out_ref[m * count:(m + 1) * count, :]


def normal(value):
    mean = jnp.mean(value, axis=-1, keepdims=True)
    centred = value - mean
    scale = lax.rsqrt(jnp.mean(centred * centred, axis=-1, keepdims=True) + EPSILON)
    return centred * scale, scale


def normal_back(grad, unit, scale, gain):
    inner = grad * gain
    return scale * (
        inner - jnp.mean(inner, axis=-1, keepdims=True) - unit * jnp.mean(inner * unit, axis=-1, keepdims=True)
    )


def error_function(x):
    x = jnp.clip(x, -4.0, 4.0)
    x2 = x * x
    top = jnp.float32(-2.72614225801306e-10)
    for a in (2.77068142495902e-08, -2.10102402082508e-06, -5.69250639462346e-05, -7.34990630326855e-04,
              -2.95459980854025e-03, -1.60960333262415e-02):
        top = top * x2 + a
    low = jnp.float32(-1.45660718464996e-05)
    for b in (-2.13374055278905e-04, -1.68282697438203e-03, -7.37332916720468e-03, -1.42647390514189e-02):
        low = low * x2 + b
    return x * top / low


def load_ou(loader, refs, r, w_out, w_up):
    targets = [(0, r, lambda rows: w_out.at[rows])]
    targets += [((1 + j) * r, r, lambda rows, j=j: w_up.at[j, rows]) for j in range(4)]
    return loader.start(refs, r, targets)


def load_down(loader, refs, r, w_down):
    return loader.start(refs, r, [(0, 4 * r, lambda rows: w_down.at[rows])])


def middle_kernel(ctx, r, ready, emit, *refs):
    att_refs = refs[:ctx]
    ou_refs, d_refs = refs[ctx:ctx + 4], refs[ctx + 4:ctx + 8]
    rows_ref, back_ref, vec_ref = refs[ctx + 8:ctx + 11]
    ga_refs = refs[ctx + 11:2 * ctx + 11]
    output_ref, first_ref, own_ref, near_ref, chip_ref, far_ref, gf_ref, cross_ref = refs[2 * ctx + 11:2 * ctx + 19]
    (w_out, w_up, w_down, act_ref, slope_ref, gp_ref, dw_ref, low_ref, mid_ref, unit_ref, feed_ref, bias_ref,
     sums_ref, sems) = refs[2 * ctx + 19:]
    half_g, s, c = position()
    core = s & 1
    loader = Loader(sems)
    first = load_ou(loader, ou_refs, r, w_out, w_up)
    second = load_down(loader, d_refs, r, w_down)
    wide = att_refs[0].shape[1]
    count, width = rows_ref.shape

    def vec(i):
        return vec_ref[i:i + 1, :].astype(F32)

    def place(m):
        return pl.ds(pl.multiple_of((c ^ m) * wide, wide), wide)

    def down_rows(j):
        return pl.ds(pl.multiple_of(j * 4 * r, 4 * r), 4 * r)

    if w_out.shape[0] > width:
        w_out[width:, :] = jnp.zeros((w_out.shape[0] - width, width), BF)
    ready()
    for j in range(4):
        bias_ref[j] = vec(9 + j)
    wait_all(first)
    total = rows_ref[...].astype(F32) + vec(3)
    for m in range(ctx):
        total = total + product(att_refs[m][...], w_out[place(m), :])
    unit, scale = normal(total)
    unit_ref[...] = unit
    mid = unit * vec(4) + vec(5)
    mid_ref[...] = mid
    low = mid.astype(BF)
    low_ref[...] = low
    parts = [low[:, i * r:(i + 1) * r] for i in range(4)]
    even = jnp.concatenate([parts[0], parts[2]], axis=1)
    odd = jnp.concatenate([parts[1], parts[3]], axis=1)
    mine = jnp.where(core == 0, even, odd)
    other = jnp.where(core == 0, odd, even)
    at, top = 4 * count, count // 2
    for ref, start, value in ((own_ref, at, mine), (near_ref, at, other), (cross_ref, 2 * count, other),
                              (cross_ref, 2 * count + top, mine)):
        ref[start:start + top, :2 * r] = value[:top]
        ref[start:start + top, 2 * r:] = value[top:]

    def up(j, carry):
        pre = product(low_ref[...], w_up[j]) + bias_ref[j]
        below = 0.5 + 0.5 * error_function(pre * (0.5 ** 0.5))
        slope = below + pre * jnp.exp(-0.5 * pre * pre) * (1.0 / math.sqrt(2.0 * math.pi))
        slope_ref[j] = slope.astype(BF)
        act_ref[j] = (pre * below).astype(BF)
        return carry

    lax.fori_loop(0, 4, up, 0)
    chip_ref[...] = act_ref[s ^ 2]
    emit(ctx + 4)
    far_ref[...] = act_ref[s ^ 3]
    emit(ctx + 5)
    own_ref[:count, :] = act_ref[s]
    near_ref[:count, :] = act_ref[s ^ 1]
    wait_all(second)
    feed_ref[...] = mid_ref[...] + vec(6)

    def down(j, carry):
        feed_ref[...] += product(act_ref[j], w_down[down_rows(j), :])
        return carry

    lax.fori_loop(0, 4, down, 0)
    unit_two, scale_two = normal(feed_ref[...])
    output_ref[...] = (unit_two * vec(7) + vec(8)).astype(BF)
    emit(ctx)
    back = back_ref[...].astype(F32)
    second_sums = [column_sum(back * unit_two), column_sum(back)]
    grad_second = normal_back(back, unit_two, scale_two, vec(7))
    feed_ref[...] = grad_second
    grad_feed = grad_second.astype(BF)
    gf_ref[...] = grad_feed
    emit(ctx + 6)
    own_ref[count:2 * count, :] = grad_feed
    near_ref[count:2 * count, :] = grad_feed

    def up_back(j, carry):
        grad_pre = (slope_ref[j].astype(F32) * times_transpose(gf_ref[...], w_down[down_rows(j), :])).astype(BF)
        gp_ref[j] = grad_pre
        sums_ref[j] = column_sum(grad_pre)
        return carry

    lax.fori_loop(0, 4, up_back, 0)
    for i in range(2):
        here = gp_ref[2 * half_g + i]
        own_ref[(2 + i) * count:(3 + i) * count, :] = here
        near_ref[(2 + i) * count:(3 + i) * count, :] = here
        cross_ref[i * count:(i + 1) * count, :] = gp_ref[2 * (half_g ^ 1) + i]
    emit(ctx + 7)

    def mid_back(j, carry):
        feed_ref[...] += times_transpose(gp_ref[j], w_up[j])
        return carry

    lax.fori_loop(0, 4, mid_back, 0)
    grad_mid = feed_ref[...]
    unit = unit_ref[...]
    grad_first = normal_back(grad_mid, unit, scale, vec(4))
    first_ref[...] = grad_first
    grad_branch = grad_first.astype(BF)
    for m in range(ctx):
        ga_refs[m][...] = times_transpose(grad_branch, w_out[place(m), :]).astype(BF)
        emit(m)
    for m in range(ctx):
        dw_ref[place(m), :] = inner_rows(att_refs[m][...], grad_branch)
    extra = jnp.concatenate(
        [column_sum(grad_branch), column_sum(grad_mid * unit), column_sum(grad_mid), *second_sums, column_sum(grad_feed)]
        + [sums_ref[j] for j in range(4)] + [jnp.zeros((6, width), F32)],
        axis=0,
    ).astype(BF)
    at = 4 * count + top
    for ref, which in ((own_ref, core), (near_ref, core ^ 1)):
        for x in range(2):
            part = dw_ref[pl.ds(pl.multiple_of((2 * x + which) * r, r), r), :]
            ref[at + x * r:at + (x + 1) * r, :] = part.astype(BF)
        ref[at + 2 * r:, :] = extra


def down_grad_kernel(r, ready, emit, a0, g0, a1, g1, a2, a3, g2, g3, okeep_ref, ocame_ref, keep_ref, send_ref, dw_ref):
    half_g, _, _ = position()
    ready()
    dw_ref[...] = inner_rows(a0[...], g0[...])
    for a, g in ((a1, g1), (a2, g2), (a3, g3)):
        dw_ref[...] += inner_rows(a[...], g[...])
    half = 2 * r
    keep_ref[:half, :] = dw_ref[pl.ds(pl.multiple_of(half_g * half, half), half), :].astype(BF)
    send_ref[:half, :] = dw_ref[pl.ds(pl.multiple_of((half_g ^ 1) * half, half), half), :].astype(BF)
    low = okeep_ref[0:r // 2, :].astype(F32) + ocame_ref[0:r // 2, :].astype(F32)
    high = okeep_ref[r // 2:r, :].astype(F32) + ocame_ref[r // 2:r, :].astype(F32)
    extra = (okeep_ref[r:, :].astype(F32) + ocame_ref[r:, :].astype(F32)).astype(BF)
    keep_ref[half:half + r // 2, :] = jnp.where(half_g == 0, low, high).astype(BF)
    send_ref[half:half + r // 2, :] = jnp.where(half_g == 0, high, low).astype(BF)
    keep_ref[half + r // 2:, :] = extra
    send_ref[half + r // 2:, :] = extra


def up_grad_kernel(r, ready, emit, p0, m0, p1, m1, p2, m2, p3, m3, keep_ref, send_ref, dw_ref):
    _, s, _ = position()
    chip = s >> 1
    ready()
    top = m0.shape[0]
    for j in range(2):
        for i, (m, p) in enumerate(((m0, p0), (m1, p1), (m2, p2), (m3, p3))):
            at = 2 * j * top
            part = inner_rows(m[:, :2 * r], p[at:at + top]) + inner_rows(m[:, 2 * r:], p[at + top:at + 2 * top])
            dw_ref[j] = part if i == 0 else dw_ref[j] + part
        keep_ref[j * r:(j + 1) * r, :] = dw_ref[j, pl.ds(pl.multiple_of(chip * r, r), r), :].astype(BF)
        send_ref[j * r:(j + 1) * r, :] = dw_ref[j, pl.ds(pl.multiple_of((chip ^ 1) * r, r), r), :].astype(BF)


def qkv_grad_kernel(ctx, r, ready, emit, *refs):
    x_refs, g_refs = refs[:ctx], refs[ctx:2 * ctx]
    keep_ref, send_ref, dw_ref = refs[2 * ctx:]
    _, s, _ = position()
    core = s & 1
    ready()
    dw_ref[...] = inner_rows(x_refs[0][...], g_refs[0][...])
    bias = column_sum(g_refs[0][...])
    for m in range(1, ctx):
        dw_ref[...] += inner_rows(x_refs[m][...], g_refs[m][...])
        bias = bias + column_sum(g_refs[m][...])
    extra = jnp.concatenate([bias, jnp.zeros((15, bias.shape[1]), F32)], axis=0).astype(BF)
    for x in range(2):
        keep_ref[x * r:(x + 1) * r, :] = dw_ref[pl.ds(pl.multiple_of((2 * x + core) * r, r), r), :].astype(BF)
        send_ref[x * r:(x + 1) * r, :] = dw_ref[pl.ds(pl.multiple_of((2 * x + (core ^ 1)) * r, r), r), :].astype(BF)
    keep_ref[2 * r:, :] = extra
    send_ref[2 * r:, :] = extra


def input_grad_kernel(ctx, r, ready, emit, *refs):
    g_refs = refs[:ctx]
    piece_refs = refs[ctx:ctx + 6]
    first_ref, out_ref, w_ref, sems = refs[ctx + 6:]
    _, _, c = position()
    half = r // 2
    copies = Loader(sems).start(piece_refs, r, [(i * half, half, lambda rows, i=i: w_ref.at[i, rows]) for i in range(3)])
    count, width = first_ref.shape
    wide = g_refs[0].shape[1] // 3
    places = []
    for m in range(ctx):
        row = lax.broadcasted_iota(jnp.int32, (wide, width), 0)
        lane = lax.broadcasted_iota(jnp.int32, (wide, width), 1)
        places.append(jnp.where(lane == row + (c ^ m) * wide, 1.0, 0.0).astype(BF))
    ready()
    full = []
    for i in range(3):
        total = product(g_refs[0][:, i * wide:(i + 1) * wide], places[0])
        for m in range(1, ctx):
            total = total + product(g_refs[m][:, i * wide:(i + 1) * wide], places[m])
        full.append(total.astype(BF))
    wait_all(copies)
    total = first_ref[...]
    for i in range(3):
        total = total + times_transpose(full[i], w_ref[i])
    out_ref[...] = total


def shards(
    inputs,
    doc_lengths,
    query_weight,
    key_weight,
    value_weight,
    out_weight,
    query_bias,
    key_bias,
    value_bias,
    out_bias,
    first_gain,
    first_shift,
    up_weight,
    up_bias,
    down_weight,
    down_bias,
    second_gain,
    second_shift,
    cotangent,
):
    groups, shard_count, ctx = (lax.axis_size(name) for name in AXES)
    here_g, here_s, here_c = (lax.axis_index(name) for name in AXES)
    chip = here_s >> 1
    half_g = here_g & 1
    ctx_bits = ctx.bit_length() - 1
    group_bits = groups.bit_length() - 1

    def move(value, dg=0, ds=0, dc=0):
        pairs = []
        for g in range(groups):
            for s in range(shard_count):
                for c in range(ctx):
                    there = ((g ^ dg) * shard_count + (s ^ ds)) * ctx + (c ^ dc)
                    pairs.append(((g * shard_count + s) * ctx + c, there))
        return lax.ppermute(value, AXES, pairs)

    def in_order(blocks, index):
        bit = 1
        while bit < len(blocks):
            swap = (index & bit) != 0
            blocks = [jnp.where(swap, blocks[m ^ bit], blocks[m]) for m in range(len(blocks))]
            bit *= 2
        return blocks

    rows = inputs[0]
    count, width = rows.shape
    length = count * ctx
    hpd = -(-HEADS // ctx)
    slots = hpd * ctx
    wide = 64 * hpd
    r = query_weight.shape[0]
    half = r // 2

    def after(value, *others):
        return lax.optimization_barrier((value, others))[0]

    blocks = {0: rows}
    for b in reversed(range(ctx_bits)):
        bit = 1 << b
        blocks.update({m ^ bit: move(v, dc=bit) for m, v in list(blocks.items())})
    xs = [blocks[m] for m in range(ctx)]
    qkv_send, qkv_own, ou_own = run(
        functools.partial(pack_kernel, r),
        "pack",
        [shape((3 * half, width)), shape((2, 3 * half, width)), shape((5 * r, width))],
        (query_weight, key_weight, value_weight, out_weight, up_weight),
        "rrrrr",
        [pltpu.SemaphoreType.DMA((14,))],
    )

    def spread_out(own, first):
        second = move(first, dg=1)
        return (own, move(own, ds=1), first, second, move(first, ds=1), move(second, ds=1))

    qkv_first = move(qkv_send, ds=2)
    qkv = spread_out(qkv_own, qkv_first)
    small = jnp.concatenate(
        [after(up_bias, qkv_send), query_bias, key_bias, value_bias, out_bias, first_gain, first_shift, down_bias,
         second_gain, second_shift]
    )
    small = jnp.pad(small, (0, 16 * width - small.shape[0])).reshape(16, width)
    small_far = move(small, ds=2)
    small = (small, move(small, ds=1), small_far, move(small_far, ds=1))

    d_far = move(after(down_weight, qkv_first, small_far), ds=2)
    ou_far = move(after(ou_own, d_far, xs), ds=2)

    cosine, sine, dcol, drow = run(
        functools.partial(tables_kernel, count),
        "tables",
        [shape((length, 128), F32), shape((length, 128), F32), shape((length, 1), F32), shape((1, length), F32)],
        (after(doc_lengths, small_far),),
        "m",
    )

    steps = length // 256
    outs = run(
        functools.partial(forward_kernel, hpd, ctx, r),
        "attention_forward",
        [shape((count, wide))] * ctx
        + [shape((length, 128 * hpd)), shape((length, 128 * hpd)), shape((length, wide)), shape((16, width)),
           shape((hpd, length, length))],
        (*xs, *qkv, *small, cosine, sine, dcol, drow),
        "s" * ctx + "r" * 10 + "ssss",
        [pltpu.VMEM((hpd, length, length), BF), pltpu.VMEM((3, width, width), BF), pltpu.VMEM((64, width), BF),
         pltpu.VMEM((width, 128 * hpd), BF), pltpu.VMEM((width, 128 * hpd), BF), pltpu.VMEM((width, wide), BF),
         pltpu.VMEM((length, wide), BF), pltpu.SemaphoreType.DMA((steps,)), pltpu.SemaphoreType.DMA((28,))],
        raw_outs=(ctx + 4,),
    )
    att, (q_turned, k_turned, v_low, vec, probs) = outs[:ctx], outs[ctx:]

    def exchange_ctx(pieces):
        return [pieces[0]] + [move(pieces[m], dc=m) for m in range(1, ctx)]

    att = exchange_ctx(att)
    down = (down_weight, move(down_weight, ds=1), d_far, move(after(d_far, att), ds=1))
    ou = (ou_own, move(ou_own, ds=1), ou_far, move(after(ou_far, att), ds=1))
    tile = (count, width)
    packed = 4 * count + count // 2 + 2 * r + 16
    outs = run(
        functools.partial(middle_kernel, ctx, r),
        "middle",
        [shape((count, wide))] * ctx
        + [shape(tile), shape(tile, F32), shape((packed, width)), shape((packed, width)), shape(tile), shape(tile), shape(tile),
           shape((3 * count, width))],
        (*att, *ou, *down, rows, cotangent[0], vec),
        "s" * ctx + "r" * 8 + "sss",
        [pltpu.VMEM((max(slots * HEAD, width), width), BF), pltpu.VMEM((4, width, width), BF), pltpu.VMEM((4 * width, width), BF)]
        + [pltpu.VMEM((4, *tile), BF)] * 3
        + [pltpu.VMEM((max(slots * HEAD, width), width), F32), pltpu.VMEM(tile, BF)]
        + [pltpu.VMEM(tile, F32)] * 3 + [pltpu.VMEM((4, 1, width), F32)] * 2 + [pltpu.SemaphoreType.DMA((28,))],
    )
    grad_att, (output, grad_first, own, near_send, chip_send, far_send, grad_feed, cross_send) = outs[:ctx], outs[ctx:]

    def add(one, other):
        return (one.astype(F32) + other.astype(F32)).astype(BF)

    def ordered_pair(mine_part, other_part, bit_value, axis):
        low = jnp.where(bit_value == 0, mine_part, other_part)
        high = jnp.where(bit_value == 0, other_part, mine_part)
        return jnp.concatenate([low, high], axis=axis)

    def split(total, sizes, bit_value):
        keep, send = [], []
        at = 0
        for size in sizes:
            part = total[at:at + size]
            at += size
            keep.append(cut(part, bit_value * (size // 2), size // 2, 0))
            send.append(cut(part, (1 - bit_value) * (size // 2), size // 2, 0))
        rest = [total[at:]] if at < total.shape[0] else []
        return jnp.concatenate(keep + rest, axis=0), jnp.concatenate(send + rest, axis=0)

    def halve(total, sizes, bit_value, **how):
        keep, send = split(total, sizes, bit_value)
        return add(keep, move(send, **how)), [size // 2 for size in sizes]

    def double(total, sizes, bit_value, **how):
        came = move(total, **how)
        at, out = 0, []
        for size in sizes:
            out.append(ordered_pair(total[at:at + size], came[at:at + size], bit_value, 0))
            at += size
        return jnp.concatenate(out, axis=0), [2 * size for size in sizes]

    def reduce(total, sizes, steps):
        for i, (bit_value, how) in enumerate(steps):
            total = after(total, input_grad) if i == 1 else total
            total, sizes = halve(total, sizes, bit_value, **how)
        return total[:sum(sizes)], sizes, total[sum(sizes):]

    def gather(total, sizes, steps):
        for bit_value, how in reversed(steps):
            total, sizes = double(total, sizes, bit_value, **how)
        return total, sizes

    reduce_steps = [((here_g >> b) & 1, dict(dg=1 << b)) for b in range(1, group_bits)]
    reduce_steps += [((here_c >> b) & 1, dict(dc=1 << b)) for b in range(ctx_bits)]

    grad_att = exchange_ctx(grad_att)
    near = move(near_send, ds=1)
    chip_act = move(chip_send, ds=2)
    far_act = move(far_send, ds=3)
    chip_feed = move(grad_feed, ds=2)
    cross = move(cross_send, dg=1)
    mid_at = 4 * count
    o_at = mid_at + count // 2
    o_mid = add(own[o_at:], near[o_at:])
    o_keep, o_send = split(o_mid, [2 * r], chip)
    o_came = move(o_send, ds=2)

    grads = run(
        functools.partial(backward_kernel, hpd, ctx),
        "attention_backward",
        [shape((count, 3 * wide))] * ctx,
        (probs, q_turned, k_turned, v_low, cosine, after(sine, o_send), *grad_att),
        "r" + "s" * (5 + ctx),
        [pltpu.VMEM((hpd, length, length), BF), pltpu.VMEM((length, wide), BF), pltpu.VMEM((length, 3 * wide), BF),
         pltpu.VMEM((length, 128 * hpd), F32), pltpu.VMEM((length, wide), F32), pltpu.SemaphoreType.DMA((steps,))],
    )
    received = exchange_ctx(grads)
    far_feed = move(after(chip_feed, grads, chip_act, far_act, o_came), ds=1)
    cross_near = move(after(cross, grads, chip_act, far_act, o_came), ds=1)

    d_keep, d_send = run(
        functools.partial(down_grad_kernel, r),
        "down_grad",
        [shape((2 * r + half + 16, width))] * 2,
        (own, own, near, near, chip_act, far_act, chip_feed, far_feed, o_keep, after(o_came, grads)),
        [(0, count), (count, count)] * 2 + ["s"] * 6,
        scratch=[pltpu.VMEM((4 * r, width), F32)],
    )

    u_keep, u_send = run(
        functools.partial(up_grad_kernel, r),
        "up_grad",
        [shape((2 * r, width))] * 2,
        (after(own, d_keep), own, near, near, cross, cross, cross_near, cross_near),
        [(2 * count, 2 * count), (mid_at, count // 2)] * 2
        + [(0, 2 * count), (2 * count + count // 2, count // 2), (0, 2 * count), (2 * count, count // 2)],
        scratch=[pltpu.VMEM((2, 2 * r, width), F32)],
    )
    u_came = move(u_send, ds=2)
    d_came = move(after(d_send, u_keep), dg=1)

    q_keep, q_send = run(
        functools.partial(qkv_grad_kernel, ctx, r),
        "qkv_grad",
        [shape((2 * r + 16, 3 * wide))] * 2,
        (*xs, after(grads[0], u_keep), *grads[1:]),
        scratch=[pltpu.VMEM((width, 3 * wide), F32)],
    )
    total_q = add(q_keep, move(after(q_send, d_came, u_came), ds=1))
    total_q, _ = halve(total_q, [2 * r], chip, ds=2)
    total_d = add(d_keep, d_came)
    total_u = add(u_keep, u_came)

    (input_grad,) = run(
        functools.partial(input_grad_kernel, ctx, r),
        "input_grad",
        [shape(tile, F32)],
        (*received, *qkv, grad_first),
        "s" * ctx + "r" * 6 + "s",
        [pltpu.VMEM((3, width, width), BF), pltpu.SemaphoreType.DMA((24,))],
    )

    total = jnp.concatenate([total_d[:2 * r + half], total_u, total_d[2 * r + half:]], axis=0)
    total, sizes, extra = reduce(total, [2 * r, half, 2 * r], reduce_steps)
    cut_at = sum(sizes[:2])
    total_d, total_u = total[:cut_at], total[cut_at:]
    total_d, sizes_d = gather(total_d, sizes[:2], reduce_steps)
    total_d, _ = double(total_d, sizes_d, half_g, dg=1)
    down_sum, out_sum = total_d[:4 * r].astype(F32), total_d[4 * r:].astype(F32)
    other = move(total_u, dg=1)
    low = jnp.where(half_g == 0, total_u, other)
    high = jnp.where(half_g == 0, other, total_u)
    total_u, _ = gather(jnp.concatenate([low, high], axis=0), sizes[2:] * 2, reduce_steps)
    up_sum = jnp.concatenate([total_u[i * r:(i + 1) * r] for i in range(4)], axis=1).astype(F32)

    total, _ = halve(total_q, [r], half_g, dg=1)
    for b in range(1, group_bits):
        total = add(total, move(total, dg=1 << b))
    gathered = {0: total}
    for b in reversed(range(ctx_bits)):
        bit = 1 << b
        gathered.update({m ^ bit: move(v, dc=bit) for m, v in list(gathered.items())})
    gathered = in_order([gathered[m] for m in range(ctx)], here_c)
    extra_mine = cut(extra.astype(F32), here_s * r, r, 1)

    wholes = [jnp.concatenate([g[:half + 1, i * wide:(i + 1) * wide] for g in gathered], axis=1)[:, :width] for i in range(3)]
    qkv_bias_sums = [cut(w[half].astype(F32), here_s * r, r, 0) for w in wholes]
    halves = jnp.concatenate([w[:half] for w in wholes], axis=0)
    qkv_total, _ = double(halves, [half] * 3, half_g, dg=1)
    qkv_sums = [qkv_total[i * r:(i + 1) * r].astype(F32) for i in range(3)]

    return (
        output[None],
        input_grad[None],
        qkv_sums[0],
        qkv_sums[1],
        qkv_sums[2],
        out_sum,
        qkv_bias_sums[0],
        qkv_bias_sums[1],
        qkv_bias_sums[2],
        extra_mine[0],
        extra_mine[1],
        extra_mine[2],
        up_sum,
        lax.dynamic_index_in_dim(extra, 6 + here_s, 0, keepdims=False).astype(F32),
        down_sum,
        extra_mine[5],
        extra_mine[3],
        extra_mine[4],
    )


def solution(mesh):
    vector, matrix, tokens = P("shard"), P("shard", None), P(("group", "shard"), "ctx", None)
    weights = (matrix,) * 4 + (vector,) * 6 + (matrix, vector, matrix) + (vector,) * 3
    in_specs = (tokens, P(("group", "shard"), None)) + weights + (tokens,)
    out_specs = (tokens, tokens) + weights
    return jax.shard_map(shards, mesh=mesh, in_specs=in_specs, out_specs=out_specs, check_vma=False)
```

```python
import functools
import math

import jax
import jax.numpy as jnp
from jax import lax
from jax.experimental import pallas as pl
from jax.experimental.pallas import tpu as pltpu
from jax.sharding import PartitionSpec as P

HEADS = 12
HEAD = 64
EPSILON = 1e-05
AXES = ("group", "shard", "ctx")
BF = jnp.bfloat16
F32 = jnp.float32
MIB = 1024 * 1024
WORK = {"pack": 4, "tables": 4, "attention_forward": 18, "middle": 21, "attention_backward": 15, "down_grad": 5, "up_grad": 5,
        "qkv_grad": 4, "input_grad": 30}
ANY = pl.BlockSpec(memory_space=pl.ANY)
SMEM = pl.BlockSpec(memory_space=pltpu.SMEM)


def product(left, right):
    return jnp.dot(left, right, preferred_element_type=F32)


def inner_rows(left, right):
    return lax.dot_general(left, right, (((0,), (0,)), ((), ())), preferred_element_type=F32)


def times_transpose(left, right):
    return lax.dot_general(left, right, (((1,), (1,)), ((), ())), preferred_element_type=F32)


def column_sum(value):
    return jnp.sum(value.astype(F32), axis=0, keepdims=True)


def cut(value, start, size, axis):
    return lax.dynamic_slice_in_dim(value, start, size, axis=axis)


def run(kernel, name, outs, operands, modes=None, scratch=(), raw_outs=()):
    modes = modes or "s" * len(operands)
    staged = [i for i, m in enumerate(modes) if m not in ("r", "m")]
    parts = [modes[i] if isinstance(modes[i], tuple) else (0, operands[i].shape[0]) for i in staged]
    held = [i for i in range(len(outs)) if i not in raw_outs]
    n, k = len(operands), len(outs)

    def body(*refs):
        ins, results = list(refs[:n]), list(refs[n:n + k])
        rest = refs[n + k:]
        slots, rest = rest[:len(staged)], rest[len(staged):]
        buffers, rest = rest[:len(held)], rest[len(held):]
        in_sems, out_sems, rest = rest[0], rest[1], rest[2:]
        copies = []
        for at, i in enumerate(staged):
            source = ins[i].at[pl.ds(*parts[at])] if isinstance(modes[i], tuple) else ins[i]
            copies.append(pltpu.make_async_copy(source, slots[at], in_sems.at[at]))
            copies[-1].start()
            ins[i] = slots[at]
        sent = {}

        def emit(i):
            at = held.index(i)
            sent[i] = pltpu.make_async_copy(buffers[at], refs[n + i], out_sems.at[at])
            sent[i].start()

        for at, i in enumerate(held):
            results[i] = buffers[at]
        kernel(lambda: wait_all(copies), emit, *ins, *results, *rest)
        for i in held:
            if i not in sent:
                emit(i)
        wait_all(sent.values())

    return pl.pallas_call(
        body,
        out_shape=outs,
        in_specs=[SMEM if m == "m" else pl.BlockSpec(memory_space=pl.ANY) for m in modes],
        out_specs=[ANY] * k,
        scratch_shapes=[pltpu.VMEM((rows, *operands[i].shape[1:]), operands[i].dtype) for i, (_, rows) in zip(staged, parts)]
        + [pltpu.VMEM(outs[i].shape, outs[i].dtype) for i in held]
        + [pltpu.SemaphoreType.DMA((max(len(staged), 1),)), pltpu.SemaphoreType.DMA((max(len(held), 1),))]
        + list(scratch),
        cost_estimate=pl.CostEstimate(flops=int(WORK[name] * 1.0 * 1e9), bytes_accessed=1, transcendentals=0),
        compiler_params=pltpu.CompilerParams(vmem_limit_bytes=62 * MIB),
        name=name,
    )(*operands)


def wait_all(copies):
    for c in copies:
        c.wait()


def shape(dims, dtype=BF):
    return jax.ShapeDtypeStruct(tuple(dims), dtype)


def position():
    s = lax.axis_index("shard")
    return lax.axis_index("group") & 1, s, lax.axis_index("ctx")


def pack_kernel(r, ready, emit, q_ref, k_ref, v_ref, o_ref, u_ref, qkv_send, qkv_ref, ou_ref, sems):
    half_g, _, _ = position()
    half = r // 2
    width = o_ref.shape[1]
    copies = []

    def copy(src, dst):
        copies.append(pltpu.make_async_copy(src, dst, sems.at[len(copies)]))
        copies[-1].start()

    mine = pl.ds(pl.multiple_of(half_g * half, half), half)
    for i, ref in enumerate((q_ref, k_ref, v_ref)):
        copy(ref.at[mine], qkv_send.at[pl.ds(i * half, half)])
    for h in range(2):
        rows = pl.ds(h * half, half)
        for i, ref in enumerate((q_ref, k_ref, v_ref)):
            copy(ref.at[rows], qkv_ref.at[h, pl.ds(i * half, half)])
    copy(o_ref, ou_ref.at[pl.ds(0, r)])
    for j in range(4):
        copy(u_ref.at[:, pl.ds(j * width, width)], ou_ref.at[pl.ds((1 + j) * r, r)])
    wait_all(copies[:3])
    emit(0)
    wait_all(copies[3:9])
    emit(1)
    wait_all(copies[9:])


class Loader:
    def __init__(self, sems):
        self.sems = sems
        self.used = 0

    def start(self, refs, r, targets):
        half_g, s, _ = position()
        if len(refs) == 4:
            copies = []
            for at, rows, target in targets:
                for i, ref in enumerate(refs):
                    start = pl.multiple_of((s ^ i) * rows, rows)
                    c = pltpu.make_async_copy(ref.at[pl.ds(at, rows)], target(pl.ds(start, rows)), self.sems.at[self.used])
                    self.used += 1
                    c.start()
                    copies.append(c)
            return copies
        own, near, first, second, near_first, near_second = refs
        pieces = [
            (own.at[0], s, 0),
            (own.at[1], s, 1),
            (near.at[0], s ^ 1, 0),
            (near.at[1], s ^ 1, 1),
            (first, s ^ 2, half_g),
            (second, s ^ 2, half_g ^ 1),
            (near_first, s ^ 3, half_g),
            (near_second, s ^ 3, half_g ^ 1),
        ]
        copies = []
        for at, rows, target in targets:
            for ref, shard, half in pieces:
                start = pl.multiple_of(shard * 2 * rows + half * rows, rows)
                c = pltpu.make_async_copy(ref.at[pl.ds(at, rows)], target(pl.ds(start, rows)), self.sems.at[self.used])
                self.used += 1
                c.start()
                copies.append(c)
        return copies


def tables_kernel(count, ready, emit, lengths_ref, cos_ref, sin_ref, dcol_ref, drow_ref):
    _, _, c = position()
    starts = []
    at = jnp.int32(0)
    for j in range(lengths_ref.shape[1]):
        starts.append(at)
        at = at + lengths_ref[0, j]

    def locate(place):
        number = jnp.zeros(place.shape, jnp.int32)
        first = jnp.zeros(place.shape, jnp.int32)
        for start in starts:
            past = start <= place
            number = number + jnp.where(past, 1, 0)
            first = jnp.maximum(first, jnp.where(past, start, 0))
        return number, first

    blocks = cos_ref.shape[0] // count
    lane = lax.broadcasted_iota(jnp.int32, (1, 128), 1)
    freqs = jnp.exp(((lane % HEAD) // 2).astype(F32) * (-2.0 / HEAD * math.log(10000.0)))
    sign = jnp.where(lane < HEAD, 1.0, -1.0)
    for m in range(blocks):
        base = (c ^ m) * count
        spot = base + lax.broadcasted_iota(jnp.int32, (count, 128), 0)
        number, first = locate(spot)
        dcol_ref[m * count:(m + 1) * count, :] = number[:, :1].astype(F32)
        angles = (spot - first).astype(F32) * freqs
        cos_ref[m * count:(m + 1) * count, :] = jnp.cos(angles)
        sin_ref[m * count:(m + 1) * count, :] = jnp.sin(angles) * sign
        across = base + lax.broadcasted_iota(jnp.int32, (1, count), 1)
        drow_ref[:, m * count:(m + 1) * count] = locate(across)[0].astype(F32)


def spread_of(rows, hpd, group):
    row = lax.broadcasted_iota(jnp.int32, (rows, 128 * hpd), 0) - group * (64 * hpd)
    lane = lax.broadcasted_iota(jnp.int32, (rows, 128 * hpd), 1)
    column = (lane // 128) * 64 + lane % 64
    odd = lane % 2
    swapped = lane % 128 >= 64
    partner = column + 1 - 2 * odd
    plain = jnp.where(swapped, 0.0, jnp.where(row == column, 1.0, 0.0))
    turned = jnp.where(swapped, jnp.where(row == partner, jnp.where(odd == 1, 1.0, -1.0), 0.0), 0.0)
    return (plain + turned).astype(BF)


def pick_of(rows, wide, group):
    row = lax.broadcasted_iota(jnp.int32, (rows, wide), 0)
    lane = lax.broadcasted_iota(jnp.int32, (rows, wide), 1)
    return jnp.where(row == lane + group * wide, 1.0, 0.0).astype(BF)


def forward_kernel(hpd, ctx, r, ready, emit, *refs):
    x_refs = refs[:ctx]
    piece_refs = refs[ctx:ctx + 6]
    small_refs = refs[ctx + 6:ctx + 10]
    cos_ref, sin_ref, dcol_ref, drow_ref = refs[ctx + 10:ctx + 14]
    att_refs = refs[ctx + 14:2 * ctx + 14]
    (q_ref, k_ref, v_ref, vec_ref, probs_out, probs_ref, w_ref, small_ref, wq_ref, wk_ref, wv_ref, att_ref, probs_sems,
     sems) = refs[2 * ctx + 14:]
    _, s, c = position()
    half = r // 2
    count, width = x_refs[0].shape
    length = count * ctx
    loader = Loader(sems)
    small = loader.start(small_refs, 16, [(0, 16, lambda rows: small_ref.at[rows])])
    copies = loader.start(piece_refs, r, [(i * half, half, lambda rows, i=i: w_ref.at[i, rows]) for i in range(3)])
    spread = spread_of(width, hpd, c)
    pick = pick_of(width, 64 * hpd, c)
    wait_all(small)
    per_row = width // r
    lines = []
    for i in range(9):
        parts = [
            small_ref[pl.ds(16 * p + 1 + i // per_row, 1), r * (i % per_row):r * (i % per_row) + r].astype(F32)
            for p in range(4)
        ]
        lines.append(jnp.concatenate(parts, axis=1))
    lines += [small_ref[pl.ds(16 * p, 1), :].astype(F32) for p in range(4)]
    lines.append(jnp.zeros((3, width), F32))
    vec = jnp.concatenate(lines, axis=0).astype(BF)
    vec_ref[...] = vec
    bq = product(vec, spread)[0:1]
    bk = product(vec, spread)[1:2]
    bv = product(vec, pick)[2:3]
    wait_all(copies)
    wq_ref[...] = product(w_ref[0], spread).astype(BF)
    wk_ref[...] = product(w_ref[1], spread).astype(BF)
    wv_ref[...] = product(w_ref[2], pick).astype(BF)
    ready()
    for m in range(ctx):
        rows = slice(m * count, (m + 1) * count)
        x = x_refs[m][...]
        for h in range(hpd):
            lanes = slice(128 * h, 128 * h + 128)
            for weight, bias, out in ((wq_ref, bq, q_ref), (wk_ref, bk, k_ref)):
                y = product(x, weight[:, lanes]) + bias[:, lanes]
                out[rows, lanes] = (y * cos_ref[rows, :] + pltpu.roll(y, 64, 1) * sin_ref[rows, :]).astype(BF)
        v_ref[rows, :] = (product(x, wv_ref[...]) + bv).astype(BF)

    once = 256

    def attend(step, carry):
        rows = pl.ds(pl.multiple_of(step * once, once), once)
        same = dcol_ref[rows, :] == drow_ref[...]
        for h in range(hpd):
            lanes = slice(128 * h, 128 * h + 128)
            scores = times_transpose(q_ref[rows, lanes], k_ref[:, lanes]) * (0.5 * HEAD ** (-0.5))
            scores = jnp.where(same, scores, -jnp.inf)
            peak = jnp.max(scores, axis=1, keepdims=True)
            expo = jnp.exp(scores - peak)
            total = jnp.sum(expo, axis=1, keepdims=True)
            probs = (expo * (1.0 / total)).astype(BF)
            probs_ref[h, rows, :] = probs
            att_ref[rows, 64 * h:64 * h + 64] = product(probs, v_ref[:, 64 * h:64 * h + 64]).astype(BF)
        probs_copy(step).start()
        return carry

    def probs_copy(step):
        rows = pl.ds(pl.multiple_of(step * once, once), once)
        return pltpu.make_async_copy(probs_ref.at[:, rows], probs_out.at[:, rows], probs_sems.at[step])

    for i in range(ctx, ctx + 4):
        emit(i)
    lax.fori_loop(0, length // once, attend, 0)
    for m in range(ctx):
        att_refs[m][...] = att_ref[m * count:(m + 1) * count, :]
        emit(m)
    for step in range(length // once):
        probs_copy(step).wait()


def backward_kernel(hpd, ctx, ready, emit, *refs):
    probs_in, q_ref, k_ref, v_ref, cos_ref, sin_ref = refs[:6]
    grad_refs = refs[6:6 + ctx]
    out_refs = refs[6 + ctx:6 + 2 * ctx]
    probs_ref, grad_ref, out_ref, gk_ref, gv_ref, probs_sems = refs[6 + 2 * ctx:]
    length = q_ref.shape[0]
    count = length // ctx
    once = 256
    factor = HEAD ** (-0.5)

    def probs_copy(step):
        rows = pl.ds(pl.multiple_of(step * once, once), once)
        return pltpu.make_async_copy(probs_in.at[:, rows], probs_ref.at[:, rows], probs_sems.at[step])

    for step in range(length // once):
        probs_copy(step).start()
    ready()
    for m in range(ctx):
        grad_ref[m * count:(m + 1) * count, :] = grad_refs[m][...]
    gk_ref[...] = jnp.zeros_like(gk_ref)
    gv_ref[...] = jnp.zeros_like(gv_ref)

    def step_of(step, carry):
        rows = pl.ds(pl.multiple_of(step * once, once), once)
        probs_copy(step).wait()
        for h in range(hpd):
            lanes = slice(128 * h, 128 * h + 128)
            narrow = slice(64 * h, 64 * h + 64)
            low = probs_ref[h, rows, :]
            probs = low.astype(F32)
            grad = grad_ref[rows, narrow]
            grad_probs = times_transpose(grad, v_ref[:, narrow])
            inner = jnp.sum(probs * grad_probs, axis=1, keepdims=True)
            grad_scores = (probs * (grad_probs - inner)).astype(BF)
            turned = product(grad_scores, k_ref[:, lanes]) * factor
            back = turned * cos_ref[rows, :] - pltpu.roll(turned, 64, 1) * sin_ref[rows, :]
            out_ref[rows, narrow] = back[:, :64].astype(BF)
            gk_ref[:, lanes] += inner_rows(grad_scores, q_ref[rows, lanes])
            gv_ref[:, narrow] += inner_rows(low, grad)
        return carry

    lax.fori_loop(0, length // once, step_of, 0)
    for h in range(hpd):
        turned = gk_ref[:, 128 * h:128 * h + 128] * factor
        back = turned * cos_ref[...] - pltpu.roll(turned, 64, 1) * sin_ref[...]
        out_ref[:, 64 * (hpd + h):64 * (hpd + h) + 64] = back[:, :64].astype(BF)
    out_ref[:, 128 * hpd:192 * hpd] = gv_ref[...].astype(BF)
    for m in range(ctx):
        out_refs[m][...] = out_ref[m * count:(m + 1) * count, :]


def normal(value):
    mean = jnp.mean(value, axis=-1, keepdims=True)
    centred = value - mean
    scale = lax.rsqrt(jnp.mean(centred * centred, axis=-1, keepdims=True) + EPSILON)
    return centred * scale, scale


def normal_back(grad, unit, scale, gain):
    inner = grad * gain
    return scale * (
        inner - jnp.mean(inner, axis=-1, keepdims=True) - unit * jnp.mean(inner * unit, axis=-1, keepdims=True)
    )


def error_function(x):
    x = jnp.clip(x, -4.0, 4.0)
    x2 = x * x
    top = jnp.float32(-2.72614225801306e-10)
    for a in (2.77068142495902e-08, -2.10102402082508e-06, -5.69250639462346e-05, -7.34990630326855e-04,
              -2.95459980854025e-03, -1.60960333262415e-02):
        top = top * x2 + a
    low = jnp.float32(-1.45660718464996e-05)
    for b in (-2.13374055278905e-04, -1.68282697438203e-03, -7.37332916720468e-03, -1.42647390514189e-02):
        low = low * x2 + b
    return x * top / low


def load_ou(loader, refs, r, w_out, w_up):
    targets = [(0, r, lambda rows: w_out.at[rows])]
    targets += [((1 + j) * r, r, lambda rows, j=j: w_up.at[j, rows]) for j in range(4)]
    return loader.start(refs, r, targets)


def load_down(loader, refs, r, w_down):
    return loader.start(refs, r, [(0, 4 * r, lambda rows: w_down.at[rows])])


def middle_kernel(ctx, r, ready, emit, *refs):
    att_refs = refs[:ctx]
    ou_refs, d_refs = refs[ctx:ctx + 4], refs[ctx + 4:ctx + 8]
    rows_ref, back_ref, vec_ref = refs[ctx + 8:ctx + 11]
    ga_refs = refs[ctx + 11:2 * ctx + 11]
    output_ref, first_ref, own_ref, near_ref, chip_ref, far_ref, gf_ref, cross_ref = refs[2 * ctx + 11:2 * ctx + 19]
    (w_out, w_up, w_down, act_ref, slope_ref, gp_ref, dw_ref, low_ref, mid_ref, unit_ref, feed_ref, bias_ref,
     sums_ref, sems) = refs[2 * ctx + 19:]
    half_g, s, c = position()
    core = s & 1
    loader = Loader(sems)
    first = load_ou(loader, ou_refs, r, w_out, w_up)
    second = load_down(loader, d_refs, r, w_down)
    wide = att_refs[0].shape[1]
    count, width = rows_ref.shape

    def vec(i):
        return vec_ref[i:i + 1, :].astype(F32)

    def place(m):
        return pl.ds(pl.multiple_of((c ^ m) * wide, wide), wide)

    def down_rows(j):
        return pl.ds(pl.multiple_of(j * 4 * r, 4 * r), 4 * r)

    if w_out.shape[0] > width:
        w_out[width:, :] = jnp.zeros((w_out.shape[0] - width, width), BF)
    ready()
    for j in range(4):
        bias_ref[j] = vec(9 + j)
    wait_all(first)
    total = rows_ref[...].astype(F32) + vec(3)
    for m in range(ctx):
        total = total + product(att_refs[m][...], w_out[place(m), :])
    unit, scale = normal(total)
    unit_ref[...] = unit
    mid = unit * vec(4) + vec(5)
    mid_ref[...] = mid
    low = mid.astype(BF)
    low_ref[...] = low
    parts = [low[:, i * r:(i + 1) * r] for i in range(4)]
    even = jnp.concatenate([parts[0], parts[2]], axis=1)
    odd = jnp.concatenate([parts[1], parts[3]], axis=1)
    mine = jnp.where(core == 0, even, odd)
    other = jnp.where(core == 0, odd, even)
    at, top = 4 * count, count // 2
    for ref, start, value in ((own_ref, at, mine), (near_ref, at, other), (cross_ref, 2 * count, other),
                              (cross_ref, 2 * count + top, mine)):
        ref[start:start + top, :2 * r] = value[:top]
        ref[start:start + top, 2 * r:] = value[top:]

    def up(j, carry):
        pre = product(low_ref[...], w_up[j]) + bias_ref[j]
        below = 0.5 + 0.5 * error_function(pre * (0.5 ** 0.5))
        slope = below + pre * jnp.exp(-0.5 * pre * pre) * (1.0 / math.sqrt(2.0 * math.pi))
        slope_ref[j] = slope.astype(BF)
        act_ref[j] = (pre * below).astype(BF)
        return carry

    lax.fori_loop(0, 4, up, 0)
    chip_ref[...] = act_ref[s ^ 2]
    emit(ctx + 4)
    far_ref[...] = act_ref[s ^ 3]
    emit(ctx + 5)
    own_ref[:count, :] = act_ref[s]
    near_ref[:count, :] = act_ref[s ^ 1]
    wait_all(second)
    feed_ref[...] = mid_ref[...] + vec(6)

    def down(j, carry):
        feed_ref[...] += product(act_ref[j], w_down[down_rows(j), :])
        return carry

    lax.fori_loop(0, 4, down, 0)
    unit_two, scale_two = normal(feed_ref[...])
    output_ref[...] = (unit_two * vec(7) + vec(8)).astype(BF)
    emit(ctx)
    back = back_ref[...].astype(F32)
    second_sums = [column_sum(back * unit_two), column_sum(back)]
    grad_second = normal_back(back, unit_two, scale_two, vec(7))
    feed_ref[...] = grad_second
    grad_feed = grad_second.astype(BF)
    gf_ref[...] = grad_feed
    emit(ctx + 6)
    own_ref[count:2 * count, :] = grad_feed
    near_ref[count:2 * count, :] = grad_feed

    def up_back(j, carry):
        grad_pre = (slope_ref[j].astype(F32) * times_transpose(gf_ref[...], w_down[down_rows(j), :])).astype(BF)
        gp_ref[j] = grad_pre
        sums_ref[j] = column_sum(grad_pre)
        return carry

    lax.fori_loop(0, 4, up_back, 0)
    for i in range(2):
        here = gp_ref[2 * half_g + i]
        own_ref[(2 + i) * count:(3 + i) * count, :] = here
        near_ref[(2 + i) * count:(3 + i) * count, :] = here
        cross_ref[i * count:(i + 1) * count, :] = gp_ref[2 * (half_g ^ 1) + i]
    emit(ctx + 7)

    def mid_back(j, carry):
        feed_ref[...] += times_transpose(gp_ref[j], w_up[j])
        return carry

    lax.fori_loop(0, 4, mid_back, 0)
    grad_mid = feed_ref[...]
    unit = unit_ref[...]
    grad_first = normal_back(grad_mid, unit, scale, vec(4))
    first_ref[...] = grad_first
    grad_branch = grad_first.astype(BF)
    for m in range(ctx):
        ga_refs[m][...] = times_transpose(grad_branch, w_out[place(m), :]).astype(BF)
        emit(m)
    for m in range(ctx):
        dw_ref[place(m), :] = inner_rows(att_refs[m][...], grad_branch)
    extra = jnp.concatenate(
        [column_sum(grad_branch), column_sum(grad_mid * unit), column_sum(grad_mid), *second_sums, column_sum(grad_feed)]
        + [sums_ref[j] for j in range(4)] + [jnp.zeros((6, width), F32)],
        axis=0,
    ).astype(BF)
    at = 4 * count + top
    for ref, which in ((own_ref, core), (near_ref, core ^ 1)):
        for x in range(2):
            part = dw_ref[pl.ds(pl.multiple_of((2 * x + which) * r, r), r), :]
            ref[at + x * r:at + (x + 1) * r, :] = part.astype(BF)
        ref[at + 2 * r:, :] = extra


def down_grad_kernel(r, ready, emit, a0, g0, a1, g1, a2, a3, g2, g3, okeep_ref, ocame_ref, keep_ref, send_ref, dw_ref):
    half_g, _, _ = position()
    ready()
    dw_ref[...] = inner_rows(a0[...], g0[...])
    for a, g in ((a1, g1), (a2, g2), (a3, g3)):
        dw_ref[...] += inner_rows(a[...], g[...])
    half = 2 * r
    keep_ref[:half, :] = dw_ref[pl.ds(pl.multiple_of(half_g * half, half), half), :].astype(BF)
    send_ref[:half, :] = dw_ref[pl.ds(pl.multiple_of((half_g ^ 1) * half, half), half), :].astype(BF)
    low = okeep_ref[0:r // 2, :].astype(F32) + ocame_ref[0:r // 2, :].astype(F32)
    high = okeep_ref[r // 2:r, :].astype(F32) + ocame_ref[r // 2:r, :].astype(F32)
    extra = (okeep_ref[r:, :].astype(F32) + ocame_ref[r:, :].astype(F32)).astype(BF)
    keep_ref[half:half + r // 2, :] = jnp.where(half_g == 0, low, high).astype(BF)
    send_ref[half:half + r // 2, :] = jnp.where(half_g == 0, high, low).astype(BF)
    keep_ref[half + r // 2:, :] = extra
    send_ref[half + r // 2:, :] = extra


def up_grad_kernel(r, ready, emit, p0, m0, p1, m1, p2, m2, p3, m3, keep_ref, send_ref, dw_ref):
    _, s, _ = position()
    chip = s >> 1
    ready()
    top = m0.shape[0]
    for j in range(2):
        for i, (m, p) in enumerate(((m0, p0), (m1, p1), (m2, p2), (m3, p3))):
            at = 2 * j * top
            part = inner_rows(m[:, :2 * r], p[at:at + top]) + inner_rows(m[:, 2 * r:], p[at + top:at + 2 * top])
            dw_ref[j] = part if i == 0 else dw_ref[j] + part
        keep_ref[j * r:(j + 1) * r, :] = dw_ref[j, pl.ds(pl.multiple_of(chip * r, r), r), :].astype(BF)
        send_ref[j * r:(j + 1) * r, :] = dw_ref[j, pl.ds(pl.multiple_of((chip ^ 1) * r, r), r), :].astype(BF)


def qkv_grad_kernel(ctx, r, ready, emit, *refs):
    x_refs, g_refs = refs[:ctx], refs[ctx:2 * ctx]
    keep_ref, send_ref, dw_ref = refs[2 * ctx:]
    _, s, _ = position()
    core = s & 1
    ready()
    dw_ref[...] = inner_rows(x_refs[0][...], g_refs[0][...])
    bias = column_sum(g_refs[0][...])
    for m in range(1, ctx):
        dw_ref[...] += inner_rows(x_refs[m][...], g_refs[m][...])
        bias = bias + column_sum(g_refs[m][...])
    extra = jnp.concatenate([bias, jnp.zeros((15, bias.shape[1]), F32)], axis=0).astype(BF)
    for x in range(2):
        keep_ref[x * r:(x + 1) * r, :] = dw_ref[pl.ds(pl.multiple_of((2 * x + core) * r, r), r), :].astype(BF)
        send_ref[x * r:(x + 1) * r, :] = dw_ref[pl.ds(pl.multiple_of((2 * x + (core ^ 1)) * r, r), r), :].astype(BF)
    keep_ref[2 * r:, :] = extra
    send_ref[2 * r:, :] = extra


def input_grad_kernel(ctx, r, ready, emit, *refs):
    g_refs = refs[:ctx]
    piece_refs = refs[ctx:ctx + 6]
    first_ref, out_ref, w_ref, sems = refs[ctx + 6:]
    _, _, c = position()
    half = r // 2
    copies = Loader(sems).start(piece_refs, r, [(i * half, half, lambda rows, i=i: w_ref.at[i, rows]) for i in range(3)])
    count, width = first_ref.shape
    wide = g_refs[0].shape[1] // 3
    places = []
    for m in range(ctx):
        row = lax.broadcasted_iota(jnp.int32, (wide, width), 0)
        lane = lax.broadcasted_iota(jnp.int32, (wide, width), 1)
        places.append(jnp.where(lane == row + (c ^ m) * wide, 1.0, 0.0).astype(BF))
    ready()
    full = []
    for i in range(3):
        total = product(g_refs[0][:, i * wide:(i + 1) * wide], places[0])
        for m in range(1, ctx):
            total = total + product(g_refs[m][:, i * wide:(i + 1) * wide], places[m])
        full.append(total.astype(BF))
    wait_all(copies)
    total = first_ref[...]
    for i in range(3):
        total = total + times_transpose(full[i], w_ref[i])
    out_ref[...] = total


def shards(
    inputs,
    doc_lengths,
    query_weight,
    key_weight,
    value_weight,
    out_weight,
    query_bias,
    key_bias,
    value_bias,
    out_bias,
    first_gain,
    first_shift,
    up_weight,
    up_bias,
    down_weight,
    down_bias,
    second_gain,
    second_shift,
    cotangent,
):
    groups, shard_count, ctx = (lax.axis_size(name) for name in AXES)
    here_g, here_s, here_c = (lax.axis_index(name) for name in AXES)
    chip = here_s >> 1
    half_g = here_g & 1
    ctx_bits = ctx.bit_length() - 1
    group_bits = groups.bit_length() - 1

    def move(value, dg=0, ds=0, dc=0):
        pairs = []
        for g in range(groups):
            for s in range(shard_count):
                for c in range(ctx):
                    there = ((g ^ dg) * shard_count + (s ^ ds)) * ctx + (c ^ dc)
                    pairs.append(((g * shard_count + s) * ctx + c, there))
        return lax.ppermute(value, AXES, pairs)

    def in_order(blocks, index):
        bit = 1
        while bit < len(blocks):
            swap = (index & bit) != 0
            blocks = [jnp.where(swap, blocks[m ^ bit], blocks[m]) for m in range(len(blocks))]
            bit *= 2
        return blocks

    rows = inputs[0]
    count, width = rows.shape
    length = count * ctx
    hpd = -(-HEADS // ctx)
    slots = hpd * ctx
    wide = 64 * hpd
    r = query_weight.shape[0]
    half = r // 2

    def after(value, *others):
        return lax.optimization_barrier((value, others))[0]

    blocks = {0: rows}
    for b in reversed(range(ctx_bits)):
        bit = 1 << b
        blocks.update({m ^ bit: move(v, dc=bit) for m, v in list(blocks.items())})
    xs = [blocks[m] for m in range(ctx)]
    qkv_send, qkv_own, ou_own = run(
        functools.partial(pack_kernel, r),
        "pack",
        [shape((3 * half, width)), shape((2, 3 * half, width)), shape((5 * r, width))],
        (query_weight, key_weight, value_weight, out_weight, up_weight),
        "rrrrr",
        [pltpu.SemaphoreType.DMA((14,))],
    )

    def spread_out(own, first):
        second = move(first, dg=1)
        return (own, move(own, ds=1), first, second, move(first, ds=1), move(second, ds=1))

    qkv_first = move(qkv_send, ds=2)
    qkv = spread_out(qkv_own, qkv_first)
    small = jnp.concatenate(
        [after(up_bias, qkv_send), query_bias, key_bias, value_bias, out_bias, first_gain, first_shift, down_bias,
         second_gain, second_shift]
    )
    small = jnp.pad(small, (0, 16 * width - small.shape[0])).reshape(16, width)
    small_far = move(small, ds=2)
    small = (small, move(small, ds=1), small_far, move(small_far, ds=1))

    d_far = move(after(down_weight, qkv_first, small_far), ds=2)
    ou_far = move(after(ou_own, d_far, xs), ds=2)

    cosine, sine, dcol, drow = run(
        functools.partial(tables_kernel, count),
        "tables",
        [shape((length, 128), F32), shape((length, 128), F32), shape((length, 1), F32), shape((1, length), F32)],
        (after(doc_lengths, small_far),),
        "m",
    )

    steps = length // 256
    outs = run(
        functools.partial(forward_kernel, hpd, ctx, r),
        "attention_forward",
        [shape((count, wide))] * ctx
        + [shape((length, 128 * hpd)), shape((length, 128 * hpd)), shape((length, wide)), shape((16, width)),
           shape((hpd, length, length))],
        (*xs, *qkv, *small, cosine, sine, dcol, drow),
        "s" * ctx + "r" * 10 + "ssss",
        [pltpu.VMEM((hpd, length, length), BF), pltpu.VMEM((3, width, width), BF), pltpu.VMEM((64, width), BF),
         pltpu.VMEM((width, 128 * hpd), BF), pltpu.VMEM((width, 128 * hpd), BF), pltpu.VMEM((width, wide), BF),
         pltpu.VMEM((length, wide), BF), pltpu.SemaphoreType.DMA((steps,)), pltpu.SemaphoreType.DMA((28,))],
        raw_outs=(ctx + 4,),
    )
    att, (q_turned, k_turned, v_low, vec, probs) = outs[:ctx], outs[ctx:]

    def exchange_ctx(pieces):
        return [pieces[0]] + [move(pieces[m], dc=m) for m in range(1, ctx)]

    att = exchange_ctx(att)
    down = (down_weight, move(down_weight, ds=1), d_far, move(after(d_far, att), ds=1))
    ou = (ou_own, move(ou_own, ds=1), ou_far, move(after(ou_far, att), ds=1))
    tile = (count, width)
    packed = 4 * count + count // 2 + 2 * r + 16
    outs = run(
        functools.partial(middle_kernel, ctx, r),
        "middle",
        [shape((count, wide))] * ctx
        + [shape(tile), shape(tile, F32), shape((packed, width)), shape((packed, width)), shape(tile), shape(tile), shape(tile),
           shape((3 * count, width))],
        (*att, *ou, *down, rows, cotangent[0], vec),
        "s" * ctx + "r" * 8 + "sss",
        [pltpu.VMEM((max(slots * HEAD, width), width), BF), pltpu.VMEM((4, width, width), BF), pltpu.VMEM((4 * width, width), BF)]
        + [pltpu.VMEM((4, *tile), BF)] * 3
        + [pltpu.VMEM((max(slots * HEAD, width), width), F32), pltpu.VMEM(tile, BF)]
        + [pltpu.VMEM(tile, F32)] * 3 + [pltpu.VMEM((4, 1, width), F32)] * 2 + [pltpu.SemaphoreType.DMA((28,))],
    )
    grad_att, (output, grad_first, own, near_send, chip_send, far_send, grad_feed, cross_send) = outs[:ctx], outs[ctx:]

    def add(one, other):
        return (one.astype(F32) + other.astype(F32)).astype(BF)

    def ordered_pair(mine_part, other_part, bit_value, axis):
        low = jnp.where(bit_value == 0, mine_part, other_part)
        high = jnp.where(bit_value == 0, other_part, mine_part)
        return jnp.concatenate([low, high], axis=axis)

    def split(total, sizes, bit_value):
        keep, send = [], []
        at = 0
        for size in sizes:
            part = total[at:at + size]
            at += size
            keep.append(cut(part, bit_value * (size // 2), size // 2, 0))
            send.append(cut(part, (1 - bit_value) * (size // 2), size // 2, 0))
        rest = [total[at:]] if at < total.shape[0] else []
        return jnp.concatenate(keep + rest, axis=0), jnp.concatenate(send + rest, axis=0)

    def halve(total, sizes, bit_value, **how):
        keep, send = split(total, sizes, bit_value)
        return add(keep, move(send, **how)), [size // 2 for size in sizes]

    def double(total, sizes, bit_value, **how):
        came = move(total, **how)
        at, out = 0, []
        for size in sizes:
            out.append(ordered_pair(total[at:at + size], came[at:at + size], bit_value, 0))
            at += size
        return jnp.concatenate(out, axis=0), [2 * size for size in sizes]

    def reduce(total, sizes, steps):
        for i, (bit_value, how) in enumerate(steps):
            total = after(total, input_grad) if i == 1 else total
            total, sizes = halve(total, sizes, bit_value, **how)
        return total[:sum(sizes)], sizes, total[sum(sizes):]

    def gather(total, sizes, steps):
        for bit_value, how in reversed(steps):
            total, sizes = double(total, sizes, bit_value, **how)
        return total, sizes

    reduce_steps = [((here_g >> b) & 1, dict(dg=1 << b)) for b in range(1, group_bits)]
    reduce_steps += [((here_c >> b) & 1, dict(dc=1 << b)) for b in range(ctx_bits)]

    grad_att = exchange_ctx(grad_att)
    near = move(near_send, ds=1)
    chip_act = move(chip_send, ds=2)
    far_act = move(far_send, ds=3)
    chip_feed = move(grad_feed, ds=2)
    cross = move(cross_send, dg=1)
    mid_at = 4 * count
    o_at = mid_at + count // 2
    o_mid = add(own[o_at:], near[o_at:])
    o_keep, o_send = split(o_mid, [2 * r], chip)
    o_came = move(o_send, ds=2)

    grads = run(
        functools.partial(backward_kernel, hpd, ctx),
        "attention_backward",
        [shape((count, 3 * wide))] * ctx,
        (probs, q_turned, k_turned, v_low, cosine, after(sine, o_send), *grad_att),
        "r" + "s" * (5 + ctx),
        [pltpu.VMEM((hpd, length, length), BF), pltpu.VMEM((length, wide), BF), pltpu.VMEM((length, 3 * wide), BF),
         pltpu.VMEM((length, 128 * hpd), F32), pltpu.VMEM((length, wide), F32), pltpu.SemaphoreType.DMA((steps,))],
    )
    received = exchange_ctx(grads)
    far_feed = move(after(chip_feed, grads, chip_act, far_act, o_came), ds=1)
    cross_near = move(after(cross, grads, chip_act, far_act, o_came), ds=1)

    d_keep, d_send = run(
        functools.partial(down_grad_kernel, r),
        "down_grad",
        [shape((2 * r + half + 16, width))] * 2,
        (own, own, near, near, chip_act, far_act, chip_feed, far_feed, o_keep, after(o_came, grads)),
        [(0, count), (count, count)] * 2 + ["s"] * 6,
        scratch=[pltpu.VMEM((4 * r, width), F32)],
    )

    u_keep, u_send = run(
        functools.partial(up_grad_kernel, r),
        "up_grad",
        [shape((2 * r, width))] * 2,
        (after(own, d_keep), own, near, near, cross, cross, cross_near, cross_near),
        [(2 * count, 2 * count), (mid_at, count // 2)] * 2
        + [(0, 2 * count), (2 * count + count // 2, count // 2), (0, 2 * count), (2 * count, count // 2)],
        scratch=[pltpu.VMEM((2, 2 * r, width), F32)],
    )
    u_came = move(u_send, ds=2)
    d_came = move(after(d_send, u_keep), dg=1)

    q_keep, q_send = run(
        functools.partial(qkv_grad_kernel, ctx, r),
        "qkv_grad",
        [shape((2 * r + 16, 3 * wide))] * 2,
        (*xs, after(grads[0], u_keep), *grads[1:]),
        scratch=[pltpu.VMEM((width, 3 * wide), F32)],
    )
    total_q = add(q_keep, move(after(q_send, d_came, u_came), ds=1))
    total_q, _ = halve(total_q, [2 * r], chip, ds=2)
    total_d = add(d_keep, d_came)
    total_u = add(u_keep, u_came)

    (input_grad,) = run(
        functools.partial(input_grad_kernel, ctx, r),
        "input_grad",
        [shape(tile, F32)],
        (*received, *qkv, grad_first),
        "s" * ctx + "r" * 6 + "s",
        [pltpu.VMEM((3, width, width), BF), pltpu.SemaphoreType.DMA((24,))],
    )

    total = jnp.concatenate([total_d[:2 * r + half], total_u, total_d[2 * r + half:]], axis=0)
    total, sizes, extra = reduce(total, [2 * r, half, 2 * r], reduce_steps)
    cut_at = sum(sizes[:2])
    total_d, total_u = total[:cut_at], total[cut_at:]
    total_d, sizes_d = gather(total_d, sizes[:2], reduce_steps)
    total_d, _ = double(total_d, sizes_d, half_g, dg=1)
    down_sum, out_sum = total_d[:4 * r].astype(F32), total_d[4 * r:].astype(F32)
    other = move(total_u, dg=1)
    low = jnp.where(half_g == 0, total_u, other)
    high = jnp.where(half_g == 0, other, total_u)
    total_u, _ = gather(jnp.concatenate([low, high], axis=0), sizes[2:] * 2, reduce_steps)
    up_sum = jnp.concatenate([total_u[i * r:(i + 1) * r] for i in range(4)], axis=1).astype(F32)

    total, _ = halve(total_q, [r], half_g, dg=1)
    for b in range(1, group_bits):
        total = add(total, move(total, dg=1 << b))
    gathered = {0: total}
    for b in reversed(range(ctx_bits)):
        bit = 1 << b
        gathered.update({m ^ bit: move(v, dc=bit) for m, v in list(gathered.items())})
    gathered = in_order([gathered[m] for m in range(ctx)], here_c)
    extra_mine = cut(extra.astype(F32), here_s * r, r, 1)

    wholes = [jnp.concatenate([g[:half + 1, i * wide:(i + 1) * wide] for g in gathered], axis=1)[:, :width] for i in range(3)]
    qkv_bias_sums = [cut(w[half].astype(F32), here_s * r, r, 0) for w in wholes]
    halves = jnp.concatenate([w[:half] for w in wholes], axis=0)
    qkv_total, _ = double(halves, [half] * 3, half_g, dg=1)
    qkv_sums = [qkv_total[i * r:(i + 1) * r].astype(F32) for i in range(3)]

    return (
        output[None],
        input_grad[None],
        qkv_sums[0],
        qkv_sums[1],
        qkv_sums[2],
        out_sum,
        qkv_bias_sums[0],
        qkv_bias_sums[1],
        qkv_bias_sums[2],
        extra_mine[0],
        extra_mine[1],
        extra_mine[2],
        up_sum,
        lax.dynamic_index_in_dim(extra, 6 + here_s, 0, keepdims=False).astype(F32),
        down_sum,
        extra_mine[5],
        extra_mine[3],
        extra_mine[4],
    )


def solution(mesh):
    vector, matrix, tokens = P("shard"), P("shard", None), P(("group", "shard"), "ctx", None)
    weights = (matrix,) * 4 + (vector,) * 6 + (matrix, vector, matrix) + (vector,) * 3
    in_specs = (tokens, P(("group", "shard"), None)) + weights + (tokens,)
    out_specs = (tokens, tokens) + weights
    return jax.shard_map(shards, mesh=mesh, in_specs=in_specs, out_specs=out_specs, check_vma=False)
```
